256 devices in a mesh: comp: 2 (over core), lat: 32 (over y, z), lon: 4 (over x).
Axes of the slice: x: 4, y: 4, z: 8, core: 2. Of those that a mesh axis runs over, the one named last changes fastest.
Arguments:
- increment: float32 [2, 8, 512, 2048], P('comp', None, 'lat', 'lon'), may hold values from -6 to 6
- diffusivity: float32 [2, 8, 512, 2048], P('comp', None, 'lat', 'lon'), may hold values from 0.03 to 0.24
- innovation: float32 [2, 8, 512, 2048], P('comp', None, 'lat', 'lon'), may hold values from -6 to 6
- land_mask: int32 [512, 2048], P('lat', 'lon'), may hold values 0 or 1
- pull_cells: int32 [2, 32, 4, 32, 1024], P('comp', 'lat', 'lon'), may hold values from 0 to 8191
- put_cells: int32 [2, 32, 4, 32, 1024], P('comp', 'lat', 'lon'), may hold values from 0 to 8191
- pull_weight: float32 [2, 32, 4, 32, 1024], P('comp', 'lat', 'lon'), may hold values from 0.2 to 0.8
- pull_count: int32 [2, 32, 4, 32], P('comp', 'lat', 'lon'), may hold values from 1 to 1024, 16384 in all within a row
Outputs:
- linear_state: float32 [2, 8, 512, 2048], P('comp', None, 'lat', 'lon')
- gradient: float32 [2, 8, 512, 2048], P('comp', None, 'lat', 'lon')
The draws below stay inside these ranges and needn't reach their ends.
Inputs may be any that keep to these rules, and one draw needn't show every extreme that they name: `pull_count`: for each receiving block the counts over the 32 source bands add up to 16384, and the largest of them is 1024.
All inputs are finite; a program needn't handle non-finite values. No bound on the sum of `land_mask` on one device may be relied on, other than what follows from the above.
Results may differ from the reference program's by a relative error of at most 0.00002.
Values sent between devices are 32-bit elements; how exact they have to be, the bound alone decides.
No kernel may reach another device: no remote copies, remote signals or barrier semaphores. Data moves between devices by JAX's collectives and lax.ppermute only.
A program may use at most 64 MiB of HBM per device.

```python
import math
import jax
import jax.numpy as jnp
import numpy as np

CLAT = 16
CLON = 512
LEV = 8
NSTEP = 4
NLAT = 512
NLON = 2048
CAP = 1024
N_LAT = 32
N_LON = 4


def with_ends(entries, stream_key, least, largest):
    place = [jax.random.randint(jax.random.fold_in(stream_key, axis), (), 0, length) for axis, length in enumerate(entries.shape)]
    widest = entries.shape.index(max(entries.shape))
    next_to = place[:widest] + [(place[widest] + 1) % entries.shape[widest]] + place[widest + 1:]
    return entries.at[tuple(place)].set(least).at[tuple(next_to)].set(largest)


def block_levels(stream_key, extent, shards, least, largest):
    def one(axis_at, blocks):
        steps = jax.random.uniform(jax.random.fold_in(jax.random.fold_in(stream_key, 6), axis_at), (blocks,), jnp.float32, least / len(shards), largest / len(shards))
        return jnp.repeat(jnp.exp(steps), extent[axis_at] // blocks).reshape((-1,) + (1,) * (len(extent) - axis_at - 1))

    level = one(*shards[0])
    for cut in shards[1:]:
        level = level * one(*cut)
    return level


def profile(count, total, bound, lean):
    loads = [(1 << 20) // math.isqrt(grade ** lean) + 1 for grade in range(2, count + 1)]
    rest, counts = total - bound - (count - 1), [1] * (count - 1)
    while rest > 0:
        movable = [i for i in range(count - 1) if counts[i] < bound]
        pool, left = sum([loads[i] for i in movable]), rest
        for i in movable:
            extra = min(bound - counts[i], max(1, left * loads[i] // pool), rest)
            counts[i] = counts[i] + extra
            rest = rest - extra
    return np.array([bound] + counts)


def ragged(own_key, number_of, total, most, skew):
    if number_of == 2:
        one = jax.random.randint(own_key, (), max(1, total - most), min(most, total - 1) + 1)
        return jnp.stack([one, total - one])
    sizes = jnp.asarray(profile(number_of, total, most, skew), jnp.int32)
    couples = (number_of - 1) // 2
    giver, sink = sizes[1:1 + 2 * couples:2], sizes[2:2 + 2 * couples:2]
    margin = jnp.minimum(giver - 1, most - sink)
    shifted = jax.random.randint(jax.random.fold_in(own_key, 1), (couples,), 0, 1 << 20) % (margin + 1)
    sizes = sizes.at[1:1 + 2 * couples:2].set(giver - shifted).at[2:2 + 2 * couples:2].set(sink + shifted)
    return sizes[jax.random.permutation(jax.random.fold_in(own_key, 2), number_of)]


def centred(own_key, extent, width, limit, cuts=(), kind=jnp.bfloat16):
    loudness = block_levels(own_key, extent, cuts, -0.22, 0.18) if cuts else 1.0
    result = jax.random.normal(own_key, extent, jnp.float32) * width * loudness
    return jnp.minimum(jnp.maximum(result, -limit), limit).astype(kind)


def setup_inputs(seed: int = 0) -> dict:
    seeds = jax.random.split(jax.random.key(seed), 9)
    return {
        "increment": centred(seeds[0], (2, LEV, NLAT, NLON), 1.0, 6.0, ((0, 2), (2, 32), (3, 4)), jnp.float32),
        "diffusivity": jnp.clip(jnp.exp(math.log(0.24) - 2.0794415 * jax.random.uniform(seeds[1], (2, LEV, NLAT, NLON), jnp.float32) ** block_levels(seeds[1], (2, LEV, NLAT, NLON), ((0, 2), (2, 32), (3, 4)), -0.2, 0.2)), 0.03, 0.24),
        "innovation": centred(seeds[2], (2, LEV, NLAT, NLON), 1.0, 6.0, ((0, 2), (2, 32), (3, 4)), jnp.float32),
        "land_mask": with_ends((jax.random.randint(seeds[3], (NLAT, NLON), 0, 10) < 7).astype(jnp.int32), jax.random.fold_in(seeds[3], 1), 0, 1),
        "pull_cells": with_ends(jax.random.randint(seeds[4], (2, N_LAT, N_LON, N_LAT, CAP), 0, CLAT * CLON), jax.random.fold_in(seeds[4], 1), 0, (CLAT * CLON) - 1).astype(jnp.int32),
        "put_cells": with_ends(jax.random.randint(seeds[5], (2, N_LAT, N_LON, N_LAT, CAP), 0, CLAT * CLON), jax.random.fold_in(seeds[5], 1), 0, (CLAT * CLON) - 1).astype(jnp.int32),
        "pull_weight": jnp.clip(0.2 + 0.6 * jax.random.uniform(seeds[6], (2, N_LAT, N_LON, N_LAT, CAP), jnp.float32) ** block_levels(seeds[6], (2, N_LAT, N_LON, N_LAT, CAP), ((0, 2), (1, 32), (2, 4)), -0.2, 0.2), 0.2, 0.8),
        "pull_count": jax.vmap(lambda own: ragged(own, N_LAT, 2 * CLAT * CLON, CAP, 2))(jax.random.split(seeds[7], 2 * N_LAT * N_LON)).reshape((2, N_LAT, N_LON, N_LAT)).astype(jnp.int32),
    }


def beside_all(field):
    east = jnp.roll(field, -1, axis=3)
    west = jnp.roll(field, 1, axis=3)
    south = jnp.concatenate([jnp.zeros_like(field[:, :, :1, :]), field[:, :, :-1, :]], axis=2)
    folded = jnp.stack([jnp.zeros_like(field[0, :, -1, :]), field[1, :, -1, ::-1]])[:, :, None, :]
    north = jnp.concatenate([field[:, :, 1:, :], folded], axis=2)
    return (east, west, south, north)

def advance(field, coefficients):
    east, west, south, north = beside_all(field)
    change = coefficients[0] * (east - field) + coefficients[1] * (west - field)
    change = change + coefficients[2] * (south - field)
    change = change + coefficients[3] * (north - field)
    return field + change

def couple(field, mask_plane, pull_cells, put_cells, live_weight):
    cells = CLAT * CLON
    surface = mask_plane * field[:, 0]
    blocks = surface.reshape(2, N_LAT, CLAT, N_LON, CLON).transpose(0, 1, 3, 2, 4).reshape(2, N_LAT, N_LON, cells)
    source = blocks[::-1]
    comp_index = jnp.arange(2, dtype=jnp.int32)[:, None, None, None, None]
    band_index = jnp.arange(N_LAT, dtype=jnp.int32)[None, :, None, None, None]
    column_index = jnp.arange(N_LON, dtype=jnp.int32)[None, None, :, None, None]
    source_band = jnp.arange(N_LAT, dtype=jnp.int32)[None, None, None, :, None]
    values = source[comp_index, source_band, column_index, pull_cells]
    target = ((comp_index * N_LAT + band_index) * N_LON + column_index) * cells + put_cells
    income = jax.ops.segment_sum((live_weight * values).reshape(-1), target.reshape(-1), num_segments=2 * N_LAT * N_LON * cells)
    income = income.reshape(2, N_LAT, N_LON, CLAT, CLON).transpose(0, 1, 3, 2, 4).reshape(2, NLAT, NLON)
    return field.at[:, 0].add(mask_plane * income)

def reference(increment, diffusivity, innovation, land_mask, pull_cells, put_cells, pull_weight, pull_count):
    mask_plane = jnp.stack([jnp.ones((NLAT, NLON), jnp.float32), land_mask.astype(jnp.float32)])
    mask_levels = mask_plane[:, None]
    stacked = jnp.concatenate([diffusivity, mask_levels], axis=1)
    near = beside_all(stacked)
    coefficients = [mask_levels * side[:, -1:] * 0.5 * (diffusivity + side[:, :-1]) for side in near]
    live = jnp.arange(CAP, dtype=jnp.int32) < pull_count[..., None]
    live_weight = jnp.where(live, pull_weight, jnp.zeros_like(pull_weight))

    def window(field):
        for step in range(NSTEP):
            field = advance(field, coefficients)
        return couple(field, mask_plane, pull_cells, put_cells, live_weight)
    linear_state, adjoint = jax.vjp(window, increment)
    gradient = adjoint(linear_state - innovation)[0] + increment
    return (linear_state, gradient)
```

```python
import jax
import jax.numpy as jnp
from jax import lax
from jax.experimental import pallas as pl
from jax.experimental.pallas import tpu as pltpu
from jax.sharding import PartitionSpec as P

NSTEP = 4
HALO = 4
ROWS, COLS, LEV = 16, 512, 8
XR, XC = 24, 640
BANDS = 32
F32, BF16, I32 = jnp.float32, jnp.bfloat16, jnp.int32


def sds(*shape):
    return jax.ShapeDtypeStruct(shape, F32)


def call(kernel, out_shape, name, scratch=(), flops=100000, nbytes=1000000):
    return pl.pallas_call(
        kernel,
        out_shape=out_shape,
        scratch_shapes=list(scratch),
        name=name,
        cost_estimate=pl.CostEstimate(flops=flops, bytes_accessed=nbytes, transcendentals=0),
        compiler_params=pltpu.CompilerParams(vmem_limit_bytes=48 << 20),
    )


def tile_iota(dim):
    return lax.broadcasted_iota(I32, (8, 128), dim)


def up_and_fold():
    ocean = lax.axis_index("comp") == 1
    up = jnp.logical_not(ocean & (lax.axis_index("lon") >= 2))
    return up, ocean & (lax.axis_index("lat") == BANDS - 1)


def wide_iota(width, dim):
    return lax.broadcasted_iota(I32, (8, width), dim)


def put_edges(pairs, fwd_ref, bwd_ref):
    up, fold = up_and_fold()
    low = wide_iota(COLS, 0) < HALO
    sub = tile_iota(0)
    lane = tile_iota(1)
    for p, (head0, tail0, head1, tail1) in enumerate(pairs):
        head = jnp.where(low, head0, pltpu.roll(head1, HALO, 0))
        tail = jnp.where(low, pltpu.roll(tail0, HALO, 0), tail1)
        fwd_ref[p] = jnp.where(up, tail, head)
        bwd_ref[p] = jnp.where(up, head, tail)

        def mirror(ref, tail=tail, p=p):
            for k in range(4):
                x = tail[:, (3 - k) * 128 : (4 - k) * 128]
                x = jnp.where((sub & 1) == 1, pltpu.roll(x, 1, 0), pltpu.roll(x, 7, 0))
                x = jnp.where((sub & 2) == 2, pltpu.roll(x, 2, 0), pltpu.roll(x, 6, 0))
                ref[p, :, k * 128 : (k + 1) * 128] = jnp.take_along_axis(x, 127 - lane, axis=1)

        @pl.when(fold & up)
        def _():
            mirror(fwd_ref)

        @pl.when(fold & jnp.logical_not(up))
        def _():
            mirror(bwd_ref)


def take_edges(count, fwd_ref, bwd_ref):
    up, _ = up_and_fold()
    low = wide_iota(COLS, 0) < HALO
    halos = []
    for p in range((count + 1) // 2):
        a, b = fwd_ref[p], bwd_ref[p]
        north, south = jnp.where(up, b, a), jnp.where(up, a, b)
        halos.append(jnp.where(low, north, pltpu.roll(south, HALO, 0)))
        if 2 * p + 1 < count:
            halos.append(jnp.where(low, pltpu.roll(north, HALO, 0), south))
    return halos


def put_columns(tiles, east_ref, west_ref):
    lane = tile_iota(1)
    for t in range(3):
        east = jnp.zeros((8, 128), F32)
        west = jnp.zeros((8, 128), F32)
        for f, tile in enumerate(tiles):
            here = (lane >= HALO * f) & (lane < HALO * (f + 1))
            x = tile(t)
            first, last = x[:, 0:128], x[:, COLS - 128 : COLS]
            west = jnp.where(here, first if f == 0 else pltpu.roll(first, HALO * f, 1), west)
            east = jnp.where(here, pltpu.roll(last, (HALO * f + HALO) % 128, 1), east)
        east_ref[8 * t : 8 * t + 8, :] = east
        west_ref[8 * t : 8 * t + 8, :] = west


def side_column(f, from_west, from_east):
    lane = lax.broadcasted_iota(I32, (XR, 128), 1)
    east = pltpu.roll(from_east, lax.rem(128 - HALO * f, 128), 1)
    west = pltpu.roll(from_west, lax.rem(124 - HALO * f + 128, 128), 1)
    return jnp.where(lane < HALO, east, jnp.where(lane >= 128 - HALO, west, jnp.zeros_like(east)))


def extend(main, halo, side):
    return jnp.concatenate([jnp.concatenate([main, halo], axis=0), side], axis=1)


def to_east(x):
    return pltpu.roll(x, XC - 1, 1)


def to_west(x):
    return pltpu.roll(x, 1, 1)


def to_north(x):
    return pltpu.roll(x, XR - 1, 0)


def to_south(x):
    return pltpu.roll(x, 1, 0)


def sweep(f, c_east, c_north):
    c_west, c_south = to_west(c_east), to_south(c_north)
    for _ in range(NSTEP):
        change = c_east * (to_east(f) - f) + c_west * (to_west(f) - f)
        change = change + c_south * (to_south(f) - f)
        change = change + c_north * (to_north(f) - f)
        f = f + change
    return f


def first_pack(inc_ref, diff_ref, land_ref, fwd_ref, bwd_ref, mask_ref):
    ocean = lax.axis_index("comp") == 1
    mask = jnp.where(ocean, land_ref[...].astype(F32), jnp.ones((ROWS, COLS), F32))
    mask_ref[...] = mask
    heads = [inc_ref[l, 0:8, :] for l in range(LEV)] + [diff_ref[l, 0:8, :] for l in range(LEV)]
    tails = [inc_ref[l, 8:16, :] for l in range(LEV)] + [diff_ref[l, 8:16, :] for l in range(LEV)]
    heads += [mask[0:8], mask[0:8]]
    tails += [mask[8:16], mask[8:16]]
    pairs = [(heads[2 * p], tails[2 * p], heads[2 * p + 1], tails[2 * p + 1]) for p in range(LEV + 1)]
    put_edges(pairs, fwd_ref, bwd_ref)


def first_columns(inc_ref, diff_ref, mask_ref, fwd_ref, bwd_ref, halo_ref, east_ref, west_ref):
    halos = take_edges(2 * LEV + 1, fwd_ref, bwd_ref)
    for f, halo in enumerate(halos):
        halo_ref[f] = halo

    def field(f):
        def tile(t):
            if t == 2:
                return halo_ref[f]
            rows = slice(8 * t, 8 * t + 8)
            if f < LEV:
                return inc_ref[f, rows, :]
            if f < 2 * LEV:
                return diff_ref[f - LEV, rows, :]
            return mask_ref[rows, :]

        return tile

    put_columns([field(f) for f in range(2 * LEV + 1)], east_ref, west_ref)


def first_sweep(
    inc_ref, diff_ref, mask_ref, halo_ref, from_west_ref, from_east_ref,
    state_ref, ce_ref, cn_ref, surface_ref,
):
    from_west, from_east = from_west_ref[...], from_east_ref[...]
    mask = extend(mask_ref[...], halo_ref[2 * LEV], side_column(2 * LEV, from_west, from_east))
    mask_e = mask * to_east(mask) * 0.5
    mask_n = mask * to_north(mask) * 0.5

    def level(l, carry):
        diff = extend(diff_ref[l], halo_ref[LEV + l], side_column(LEV + l, from_west, from_east))
        c_east = mask_e * (diff + to_east(diff))
        c_north = mask_n * (diff + to_north(diff))
        ce_ref[l] = c_east
        cn_ref[l] = c_north
        f = extend(inc_ref[l], halo_ref[l], side_column(l, from_west, from_east))
        f = sweep(f, c_east, c_north)
        state_ref[l] = f[:ROWS, :COLS]
        return carry

    lax.fori_loop(0, LEV, level, 0)
    surface_ref[...] = mask_ref[...] * state_ref[0]


def gather_slots(table, cells):
    highs = [lax.shift_right_logical(c, 7) for c in cells]
    lows = [c & 127 for c in cells]
    found = [jnp.zeros((8, 128), F32) for _ in cells]
    for h in range(64):
        row = jnp.broadcast_to(table(h), (8, 128))
        for n in range(len(cells)):
            found[n] = jnp.where(highs[n] == h, jnp.take_along_axis(row, lows[n], axis=1), found[n])
    return found


GROUP = 8


def row_of(ref):
    return lambda h: ref[h // 4 : h // 4 + 1, (h % 4) * 128 : (h % 4) * 128 + 128]


def gather_kernel(cells_ref, table_ref, out_ref):
    def group(g, carry):
        found = gather_slots(row_of(table_ref), [cells_ref[g * GROUP + n] for n in range(GROUP)])
        for n in range(GROUP):
            out_ref[g * GROUP + n] = found[n]
        return carry

    lax.fori_loop(0, BANDS // GROUP, group, 0)


def scatter_band(cells, values):
    high_iota = lax.broadcasted_iota(I32, (64, 128), 0)
    low_iota = lax.broadcasted_iota(I32, (128, 128), 0)
    high, low = lax.shift_right_logical(cells, 7), cells & 127
    coarse = values.astype(BF16).astype(F32)
    fine = values - coarse
    left, right = [], []
    for k in range(8):
        at = high_iota == high[k : k + 1]
        a = jnp.where(at, coarse[k : k + 1], 0.0).astype(BF16)
        b = jnp.where(at, fine[k : k + 1], 0.0).astype(BF16)
        left.append(jnp.concatenate([a, b], axis=0))
        right.append(jnp.where(low_iota == low[k : k + 1], 1.0, 0.0).astype(BF16))
    return lax.dot_general(
        jnp.concatenate(left, axis=1),
        jnp.concatenate(right, axis=1),
        (((1,), (1,)), ((), ())),
        preferred_element_type=F32,
    )


def as_block(sums):
    return jnp.concatenate([sums.reshape(ROWS, 4, 128)[:, k, :] for k in range(4)], axis=1)


def sum_slots(cells_of, values_of, acc_ref):
    acc_ref[...] = jnp.zeros_like(acc_ref)

    def pair(b, carry):
        acc_ref[...] += scatter_band(cells_of(2 * b), values_of(2 * b)) + scatter_band(
            cells_of(2 * b + 1), values_of(2 * b + 1)
        )
        return carry

    lax.fori_loop(0, BANDS // 2, pair, 0)
    return as_block(acc_ref[0:64, :] + acc_ref[64:128, :])


def live_of(b, weight_ref, count_ref):
    slot = tile_iota(0) * 128 + tile_iota(1)
    return jnp.where(slot < count_ref[0, b], weight_ref[b], jnp.zeros((8, 128), F32))


def couple_kernel(
    count_ref, values_ref, cells_ref, weight_ref, mask_ref, state_ref, innov_ref,
    linear_ref, residual_ref, out_ref, acc_ref, table_ref,
):
    income = sum_slots(
        lambda b: cells_ref[b], lambda b: live_of(b, weight_ref, count_ref) * values_ref[b], acc_ref
    )
    mask = mask_ref[...]
    linear = state_ref[...] + mask * income
    residual = linear - innov_ref[...]
    linear_ref[...] = linear
    residual_ref[...] = residual
    table_ref[...] = mask * residual

    def group(g, carry):
        found = gather_slots(row_of(table_ref), [cells_ref[g * GROUP + n] for n in range(GROUP)])
        for n in range(GROUP):
            out_ref[g * GROUP + n] = live_of(g * GROUP + n, weight_ref, count_ref) * found[n]
        return carry

    lax.fori_loop(0, BANDS // GROUP, group, 0)


def collect_kernel(values_ref, cells_ref, out_ref, acc_ref):
    out_ref[...] = sum_slots(lambda b: cells_ref[b], lambda b: values_ref[b], acc_ref)


def second_pack(residual_ref, mask_ref, returned_ref, state_ref, innov_ref, adj_ref, fwd_ref, bwd_ref):
    adj_ref[0] = residual_ref[...] + mask_ref[...] * returned_ref[...]
    for l in range(1, LEV):
        adj_ref[l] = state_ref[l] - innov_ref[l]
    pairs = []
    for p in range(LEV // 2):
        a, b = 2 * p, 2 * p + 1
        pairs.append((adj_ref[a, 0:8], adj_ref[a, 8:16], adj_ref[b, 0:8], adj_ref[b, 8:16]))
    put_edges(pairs, fwd_ref, bwd_ref)


def second_columns(adj_ref, fwd_ref, bwd_ref, halo_ref, east_ref, west_ref):
    halos = take_edges(LEV, fwd_ref, bwd_ref)
    for f, halo in enumerate(halos):
        halo_ref[f] = halo

    def field(f):
        return lambda t: halo_ref[f] if t == 2 else adj_ref[f, 8 * t : 8 * t + 8, :]

    put_columns([field(f) for f in range(LEV)], east_ref, west_ref)


def second_sweep(adj_ref, halo_ref, from_west_ref, from_east_ref, ce_ref, cn_ref, inc_ref, out_ref):
    from_west, from_east = from_west_ref[...], from_east_ref[...]

    def level(l, carry):
        f = extend(adj_ref[l], halo_ref[l], side_column(l, from_west, from_east))
        f = sweep(f, ce_ref[l], cn_ref[l])
        out_ref[l] = f[:ROWS, :COLS] + inc_ref[l]
        return carry

    lax.fori_loop(0, LEV, level, 0)


def chain_pairs():
    lons = lax.axis_size("lon")

    def at(comp, lat, lon):
        return (comp * BANDS + lat) * lons + lon

    pairs = []
    for lon in range(lons):
        for lat in range(BANDS - 1):
            pairs.append((at(0, lat, lon), at(0, lat + 1, lon)))
            if lon < lons // 2:
                pairs.append((at(1, lat, lon), at(1, lat + 1, lon)))
            else:
                pairs.append((at(1, lat + 1, lon), at(1, lat, lon)))
        if lon < lons // 2:
            pairs.append((at(1, BANDS - 1, lon), at(1, BANDS - 1, lons - 1 - lon)))
    return pairs


def across(value):
    return lax.ppermute(value, "comp", [(0, 1), (1, 0)])


def along_chain(fwd, bwd):
    axes = ("comp", "lat", "lon")
    pairs = chain_pairs()
    return (
        lax.ppermute(fwd, axes, pairs),
        lax.ppermute(bwd, axes, [(b, a) for a, b in pairs]),
    )


def around(east, west):
    n = lax.axis_size("lon")
    return (
        lax.ppermute(east, "lon", [(i, (i + 1) % n) for i in range(n)]),
        lax.ppermute(west, "lon", [((i + 1) % n, i) for i in range(n)]),
    )


def exchange(slots):
    return lax.all_to_all(slots, "lat", 0, 0, tiled=True)


def local(
    increment, diffusivity, innovation, land_mask, pull_cells, put_cells, pull_weight, pull_count
):
    inc, diff, innov = increment[0], diffusivity[0], innovation[0]
    pulled = exchange(pull_cells.reshape(BANDS, 8, 128))
    placed = put_cells.reshape(BANDS, 8, 128)
    weight = pull_weight.reshape(BANDS, 8, 128)
    count = pull_count.reshape(1, BANDS)

    edge = sds(LEV + 1, 8, COLS)
    fwd, bwd, mask = call(first_pack, (edge, edge, sds(ROWS, COLS)), "first_pack")(
        inc, diff, land_mask
    )
    fwd, bwd = along_chain(fwd, bwd)
    halo, east, west = call(
        first_columns, (sds(2 * LEV + 1, 8, COLS), sds(XR, 128), sds(XR, 128)), "first_columns"
    )(inc, diff, mask, fwd, bwd)
    from_west, from_east = around(east, west)
    state, c_east, c_north, surface = call(
        first_sweep,
        (sds(LEV, ROWS, COLS), sds(LEV, XR, XC), sds(LEV, XR, XC), sds(ROWS, COLS)),
        "first_sweep",
    )(inc, diff, mask, halo, from_west, from_east)

    slots = sds(BANDS, 8, 128)
    values = exchange(call(gather_kernel, slots, "gather_slots")(pulled, across(surface)))
    acc = pltpu.VMEM((128, 128), F32)
    plane = sds(ROWS, COLS)
    smem = pl.BlockSpec(memory_space=pltpu.SMEM)
    vmem = pl.BlockSpec(memory_space=pltpu.VMEM)
    linear, residual, outgoing = pl.pallas_call(
        couple_kernel,
        out_shape=(plane, plane, slots),
        in_specs=[smem] + [vmem] * 6,
        out_specs=(vmem,) * 3,
        scratch_shapes=[acc, pltpu.VMEM((ROWS, COLS), F32)],
        name="couple",
        compiler_params=pltpu.CompilerParams(vmem_limit_bytes=48 << 20),
    )(count, values, placed, weight, mask, state[0], innov[0])
    returned = across(
        call(collect_kernel, plane, "collect", [acc])(exchange(outgoing), pulled)
    )

    edge = sds(LEV // 2, 8, COLS)
    adj, fwd, bwd = call(second_pack, (sds(LEV, ROWS, COLS), edge, edge), "second_pack")(
        residual, mask, returned, state, innov
    )
    fwd, bwd = along_chain(fwd, bwd)
    halo, east, west = call(
        second_columns, (sds(LEV, 8, COLS), sds(XR, 128), sds(XR, 128)), "second_columns"
    )(adj, fwd, bwd)
    from_west, from_east = around(east, west)
    gradient = call(second_sweep, sds(LEV, ROWS, COLS), "second_sweep")(
        adj, halo, from_west, from_east, c_east, c_north, inc
    )
    linear_state = jnp.concatenate([linear[None], state[1:]], axis=0)
    return (linear_state[None], gradient[None])


def solution(mesh):
    placed = (
        P("comp", None, "lat", "lon"),
        P("comp", None, "lat", "lon"),
        P("comp", None, "lat", "lon"),
        P("lat", "lon"),
        P("comp", "lat", "lon", None, None),
        P("comp", "lat", "lon", None, None),
        P("comp", "lat", "lon", None, None),
        P("comp", "lat", "lon", None),
    )
    return jax.shard_map(
        local,
        mesh=mesh,
        in_specs=placed,
        out_specs=(P("comp", None, "lat", "lon"), P("comp", None, "lat", "lon")),
        check_vma=False,
    )
```

```python
import jax
import jax.numpy as jnp
from jax import lax
from jax.experimental import pallas as pl
from jax.experimental.pallas import tpu as pltpu
from jax.sharding import PartitionSpec as P

NSTEP = 4
HALO = 4
ROWS, COLS, LEV = 16, 512, 8
XR, XC = 24, 640
BANDS = 32
F32, BF16, I32 = jnp.float32, jnp.bfloat16, jnp.int32


def sds(*shape):
    return jax.ShapeDtypeStruct(shape, F32)


def call(kernel, out_shape, name, scratch=(), flops=100000, nbytes=1000000):
    return pl.pallas_call(
        kernel,
        out_shape=out_shape,
        scratch_shapes=list(scratch),
        name=name,
        cost_estimate=pl.CostEstimate(flops=flops, bytes_accessed=nbytes, transcendentals=0),
        compiler_params=pltpu.CompilerParams(vmem_limit_bytes=48 << 20),
    )


def tile_iota(dim):
    return lax.broadcasted_iota(I32, (8, 128), dim)


def wide_iota(width, dim):
    return lax.broadcasted_iota(I32, (8, width), dim)


def put_edges(pairs, head_ref, tail_ref, mirror_ref):
    fold = (lax.axis_index("comp") == 1) & (lax.axis_index("lat") == BANDS - 1)
    low = wide_iota(COLS, 0) < HALO
    sub = tile_iota(0)
    lane = tile_iota(1)
    for p, (head0, tail0, head1, tail1) in enumerate(pairs):
        head_ref[p] = jnp.where(low, head0, pltpu.roll(head1, HALO, 0))
        tail = jnp.where(low, pltpu.roll(tail0, HALO, 0), tail1)
        tail_ref[p] = tail
        mirror_ref[p] = tail

    @pl.when(fold)
    def _():
        for p in range(len(pairs)):
            for k in range(4):
                x = tail_ref[p, :, (3 - k) * 128 : (4 - k) * 128]
                x = jnp.where((sub & 1) == 1, pltpu.roll(x, 1, 0), pltpu.roll(x, 7, 0))
                x = jnp.where((sub & 2) == 2, pltpu.roll(x, 2, 0), pltpu.roll(x, 6, 0))
                mirror_ref[p, :, k * 128 : (k + 1) * 128] = jnp.take_along_axis(
                    x, 127 - lane, axis=1
                )


def take_edges(count, from_south_ref, from_north_ref, from_fold_ref):
    ocean = lax.axis_index("comp") == 1
    band = lax.axis_index("lat")
    first, last = band == 0, band == BANDS - 1
    zero = jnp.zeros((8, COLS), F32)
    low = wide_iota(COLS, 0) < HALO
    halos = []
    for p in range((count + 1) // 2):
        north = jnp.where(last, jnp.where(ocean, from_fold_ref[p], zero), from_north_ref[p])
        south = jnp.where(first, zero, from_south_ref[p])
        halos.append(jnp.where(low, north, pltpu.roll(south, HALO, 0)))
        if 2 * p + 1 < count:
            halos.append(jnp.where(low, pltpu.roll(north, HALO, 0), south))
    return halos


def put_columns(tiles, east_ref, west_ref):
    lane = tile_iota(1)
    for t in range(3):
        east = jnp.zeros((8, 128), F32)
        west = jnp.zeros((8, 128), F32)
        for f, tile in enumerate(tiles):
            here = (lane >= HALO * f) & (lane < HALO * (f + 1))
            x = tile(t)
            first, last = x[:, 0:128], x[:, COLS - 128 : COLS]
            west = jnp.where(here, first if f == 0 else pltpu.roll(first, HALO * f, 1), west)
            east = jnp.where(here, pltpu.roll(last, (HALO * f + HALO) % 128, 1), east)
        east_ref[8 * t : 8 * t + 8, :] = east
        west_ref[8 * t : 8 * t + 8, :] = west


def side_column(f, from_west, from_east):
    lane = lax.broadcasted_iota(I32, (XR, 128), 1)
    east = pltpu.roll(from_east, lax.rem(128 - HALO * f, 128), 1)
    west = pltpu.roll(from_west, lax.rem(124 - HALO * f + 128, 128), 1)
    return jnp.where(lane < HALO, east, jnp.where(lane >= 128 - HALO, west, jnp.zeros_like(east)))


def extend(main, halo, side):
    return jnp.concatenate([jnp.concatenate([main, halo], axis=0), side], axis=1)


def to_east(x):
    return pltpu.roll(x, XC - 1, 1)


def to_west(x):
    return pltpu.roll(x, 1, 1)


def to_north(x):
    return pltpu.roll(x, XR - 1, 0)


def to_south(x):
    return pltpu.roll(x, 1, 0)


def sweep(f, c_east, c_north):
    c_west, c_south = to_west(c_east), to_south(c_north)
    for _ in range(NSTEP):
        change = c_east * (to_east(f) - f) + c_west * (to_west(f) - f)
        change = change + c_south * (to_south(f) - f)
        change = change + c_north * (to_north(f) - f)
        f = f + change
    return f


def first_pack(inc_ref, diff_ref, land_ref, head_ref, tail_ref, mirror_ref, mask_ref):
    ocean = lax.axis_index("comp") == 1
    mask = jnp.where(ocean, land_ref[...].astype(F32), jnp.ones((ROWS, COLS), F32))
    mask_ref[...] = mask
    heads = [inc_ref[l, 0:8, :] for l in range(LEV)] + [diff_ref[l, 0:8, :] for l in range(LEV)]
    tails = [inc_ref[l, 8:16, :] for l in range(LEV)] + [diff_ref[l, 8:16, :] for l in range(LEV)]
    heads += [mask[0:8], mask[0:8]]
    tails += [mask[8:16], mask[8:16]]
    pairs = [(heads[2 * p], tails[2 * p], heads[2 * p + 1], tails[2 * p + 1]) for p in range(LEV + 1)]
    put_edges(pairs, head_ref, tail_ref, mirror_ref)


def first_columns(
    inc_ref, diff_ref, mask_ref, from_south_ref, from_north_ref, from_fold_ref,
    halo_ref, east_ref, west_ref,
):
    halos = take_edges(2 * LEV + 1, from_south_ref, from_north_ref, from_fold_ref)
    for f, halo in enumerate(halos):
        halo_ref[f] = halo

    def field(f):
        def tile(t):
            if t == 2:
                return halo_ref[f]
            rows = slice(8 * t, 8 * t + 8)
            if f < LEV:
                return inc_ref[f, rows, :]
            if f < 2 * LEV:
                return diff_ref[f - LEV, rows, :]
            return mask_ref[rows, :]

        return tile

    put_columns([field(f) for f in range(2 * LEV + 1)], east_ref, west_ref)


def first_level(
    l, inc_ref, diff_ref, mask_ref, halo_ref, from_west, from_east, c_east_ref, c_north_ref, at
):
    mask = extend(mask_ref[...], halo_ref[2 * LEV], side_column(2 * LEV, from_west, from_east))
    diff = extend(diff_ref[l], halo_ref[LEV + l], side_column(LEV + l, from_west, from_east))
    c_east = mask * to_east(mask) * 0.5 * (diff + to_east(diff))
    c_north = mask * to_north(mask) * 0.5 * (diff + to_north(diff))
    c_east_ref[at] = c_east
    c_north_ref[at] = c_north
    f = extend(inc_ref[l], halo_ref[l], side_column(l, from_west, from_east))
    return sweep(f, c_east, c_north)[:ROWS, :COLS]


def first_surface(
    inc_ref, diff_ref, mask_ref, halo_ref, from_west_ref, from_east_ref,
    state_ref, surface_ref, c_east_ref, c_north_ref,
):
    f = first_level(
        0, inc_ref, diff_ref, mask_ref, halo_ref, from_west_ref[...], from_east_ref[...],
        c_east_ref, c_north_ref, 0,
    )
    state_ref[...] = f
    surface_ref[...] = mask_ref[...] * f


def first_rest(
    inc_ref, diff_ref, innov_ref, mask_ref, halo_ref, from_west_ref, from_east_ref,
    state_ref, adj_ref, c_east_ref, c_north_ref, head_ref, tail_ref, mirror_ref,
):
    from_west, from_east = from_west_ref[...], from_east_ref[...]

    def level(k, carry):
        f = first_level(
            k + 1, inc_ref, diff_ref, mask_ref, halo_ref, from_west, from_east,
            c_east_ref, c_north_ref, k,
        )
        state_ref[k + 1] = f
        adj_ref[k] = f - innov_ref[k + 1]
        return carry

    lax.fori_loop(0, LEV - 1, level, 0)
    state_ref[0] = jnp.zeros((ROWS, COLS), F32)
    put_edges(level_pairs(adj_ref, LEV - 1), head_ref, tail_ref, mirror_ref)


def level_pairs(ref, count):
    pairs = []
    for p in range((count + 1) // 2):
        a, b = 2 * p, min(2 * p + 1, count - 1)
        pairs.append((ref[a, 0:8], ref[a, 8:16], ref[b, 0:8], ref[b, 8:16]))
    return pairs


def row_of(ref):
    return lambda h: ref[h // 4 : h // 4 + 1, (h % 4) * 128 : (h % 4) * 128 + 128]


def gather_slots(table, cells):
    high, low = lax.shift_right_logical(cells, 7), cells & 127
    found = jnp.zeros((8, 128), F32)
    for h in range(64):
        row = jnp.broadcast_to(table(h), (8, 128))
        found = jnp.where(high == h, jnp.take_along_axis(row, low, axis=1), found)
    return found


GROUP = 8
SUMS = 4


def gather_all(cells_ref, table_ref, store):
    def group(g, carry):
        for n in range(GROUP):
            b = g * GROUP + n
            store(b, gather_slots(row_of(table_ref), cells_ref[b]))
        return carry

    lax.fori_loop(0, BANDS // GROUP, group, 0)


def gather_kernel(cells_ref, table_ref, out_ref):
    def store(b, found):
        out_ref[b] = found

    gather_all(cells_ref, table_ref, store)


def scatter_band(cells, values):
    high_iota = lax.broadcasted_iota(I32, (64, 128), 0)
    low_iota = lax.broadcasted_iota(I32, (128, 128), 0)
    high, low = lax.shift_right_logical(cells, 7), cells & 127
    coarse = values.astype(BF16).astype(F32)
    fine = values - coarse
    left, right = [], []
    for k in range(8):
        at = high_iota == high[k : k + 1]
        a = jnp.where(at, coarse[k : k + 1], 0.0).astype(BF16)
        b = jnp.where(at, fine[k : k + 1], 0.0).astype(BF16)
        left.append(jnp.concatenate([a, b], axis=0))
        right.append(jnp.where(low_iota == low[k : k + 1], 1.0, 0.0).astype(BF16))
    return lax.dot_general(
        jnp.concatenate(left, axis=1),
        jnp.concatenate(right, axis=1),
        (((1,), (1,)), ((), ())),
        preferred_element_type=F32,
    )


def as_block(sums):
    return jnp.concatenate([sums.reshape(ROWS, 4, 128)[:, k, :] for k in range(4)], axis=1)


def sum_slots(cells_of, values_of, acc_ref):
    acc_ref[...] = jnp.zeros_like(acc_ref)

    def step(g, carry):
        total = acc_ref[...]
        for n in range(SUMS):
            total = total + scatter_band(cells_of(SUMS * g + n), values_of(SUMS * g + n))
        acc_ref[...] = total
        return carry

    lax.fori_loop(0, BANDS // SUMS, step, 0)
    return as_block(acc_ref[0:64, :] + acc_ref[64:128, :])


def live_of(b, weight_ref, count_ref):
    slot = tile_iota(0) * 128 + tile_iota(1)
    return jnp.where(slot < count_ref[0, b], weight_ref[b], jnp.zeros((8, 128), F32))


def couple_kernel(
    count_ref, values_ref, cells_ref, weight_ref, mask_ref, state_ref, innov_ref,
    linear_ref, residual_ref, out_ref, acc_ref, table_ref,
):
    income = sum_slots(
        lambda b: cells_ref[b], lambda b: live_of(b, weight_ref, count_ref) * values_ref[b], acc_ref
    )
    mask = mask_ref[...]
    linear = state_ref[...] + mask * income
    residual = linear - innov_ref[...]
    linear_ref[...] = linear
    residual_ref[...] = residual
    table_ref[...] = mask * residual

    def store(b, found):
        out_ref[b] = live_of(b, weight_ref, count_ref) * found

    gather_all(cells_ref, table_ref, store)


def collect_kernel(values_ref, cells_ref, out_ref, acc_ref):
    out_ref[...] = sum_slots(lambda b: cells_ref[b], lambda b: values_ref[b], acc_ref)


def second_pack(residual_ref, mask_ref, returned_ref, adj_ref, head_ref, tail_ref, mirror_ref):
    adj_ref[0] = residual_ref[...] + mask_ref[...] * returned_ref[...]
    put_edges(level_pairs(adj_ref, 1), head_ref, tail_ref, mirror_ref)


def second_columns(
    adj_ref, from_south_ref, from_north_ref, from_fold_ref, halo_ref, east_ref, west_ref
):
    count = adj_ref.shape[0]
    halos = take_edges(count, from_south_ref, from_north_ref, from_fold_ref)
    for f, halo in enumerate(halos):
        halo_ref[f] = halo

    def field(f):
        return lambda t: halo_ref[f] if t == 2 else adj_ref[f, 8 * t : 8 * t + 8, :]

    put_columns([field(f) for f in range(count)], east_ref, west_ref)


def second_level(l, at, adj_ref, halo_ref, from_west, from_east, c_east_ref, c_north_ref, inc_ref):
    f = extend(adj_ref[at], halo_ref[at], side_column(at, from_west, from_east))
    return sweep(f, c_east_ref[at], c_north_ref[at])[:ROWS, :COLS] + inc_ref[l]


def second_rest(
    adj_ref, halo_ref, from_west_ref, from_east_ref, c_east_ref, c_north_ref, inc_ref, out_ref
):
    from_west, from_east = from_west_ref[...], from_east_ref[...]

    def level(k, carry):
        out_ref[k + 1] = second_level(
            k + 1, k, adj_ref, halo_ref, from_west, from_east, c_east_ref, c_north_ref, inc_ref
        )
        return carry

    lax.fori_loop(0, LEV - 1, level, 0)
    out_ref[0] = jnp.zeros((ROWS, COLS), F32)


def second_surface(
    adj_ref, halo_ref, from_west_ref, from_east_ref, c_east_ref, c_north_ref, inc_ref, rest_ref,
    out_ref,
):
    out_ref[...] = rest_ref[...]
    out_ref[0] = second_level(
        0, 0, adj_ref, halo_ref, from_west_ref[...], from_east_ref[...], c_east_ref, c_north_ref,
        inc_ref,
    )


def across(value):
    return lax.ppermute(value, "comp", [(0, 1), (1, 0)])


def along(head, tail, mirror):
    n, m = lax.axis_size("lat"), lax.axis_size("lon")
    return (
        lax.ppermute(tail, "lat", [(i, (i + 1) % n) for i in range(n)]),
        lax.ppermute(head, "lat", [((i + 1) % n, i) for i in range(n)]),
        lax.ppermute(mirror, "lon", [(i, m - 1 - i) for i in range(m)]),
    )


def around(east, west):
    n = lax.axis_size("lon")
    return (
        lax.ppermute(east, "lon", [(i, (i + 1) % n) for i in range(n)]),
        lax.ppermute(west, "lon", [((i + 1) % n, i) for i in range(n)]),
    )


def exchange(slots):
    return lax.all_to_all(slots, "lat", 0, 0, tiled=True)


def local(
    increment, diffusivity, innovation, land_mask, pull_cells, put_cells, pull_weight, pull_count
):
    inc, diff, innov = increment[0], diffusivity[0], innovation[0]
    pulled = exchange(pull_cells.reshape(BANDS, 8, 128))
    placed = put_cells.reshape(BANDS, 8, 128)
    weight = pull_weight.reshape(BANDS, 8, 128)
    count = pull_count.reshape(1, BANDS)

    edge = sds(LEV + 1, 8, COLS)
    packed = sds(XR, 128)
    plane = sds(ROWS, COLS)
    slots = sds(BANDS, 8, 128)
    *edges, mask = call(first_pack, (edge, edge, edge, plane), "first_pack")(inc, diff, land_mask)
    halo, east, west = call(
        first_columns, (sds(2 * LEV + 1, 8, COLS), packed, packed), "first_columns"
    )(inc, diff, mask, *along(*edges))
    from_west, from_east = around(east, west)
    wide = sds(1, XR, XC)
    state0, surface, c_east0, c_north0 = call(
        first_surface, (plane, plane, wide, wide), "first_surface"
    )(inc, diff, mask, halo, from_west, from_east)
    sent = call(gather_kernel, slots, "gather_slots")(pulled, across(surface))
    sent, halo, from_west, from_east = lax.optimization_barrier((sent, halo, from_west, from_east))
    values = exchange(sent)

    edge = sds(LEV // 2, 8, COLS)
    wide = sds(LEV - 1, XR, XC)
    state, adj, c_east, c_north, *edges = call(
        first_rest,
        (sds(LEV, ROWS, COLS), sds(LEV - 1, ROWS, COLS), wide, wide, edge, edge, edge),
        "first_rest",
        nbytes=12000000,
    )(inc, diff, innov, mask, halo, from_west, from_east)
    edges = along(*edges)

    acc = pltpu.VMEM((128, 128), F32)
    smem = pl.BlockSpec(memory_space=pltpu.SMEM)
    vmem = pl.BlockSpec(memory_space=pltpu.VMEM)
    linear, residual, outgoing = pl.pallas_call(
        couple_kernel,
        out_shape=(plane, plane, slots),
        in_specs=[smem] + [vmem] * 6,
        out_specs=(vmem,) * 3,
        scratch_shapes=[acc, pltpu.VMEM((ROWS, COLS), F32)],
        name="couple",
        compiler_params=pltpu.CompilerParams(vmem_limit_bytes=48 << 20),
    )(count, values, placed, weight, mask, state0, innov[0])

    outgoing, adj, *edges = lax.optimization_barrier((outgoing, adj, *edges))
    back = exchange(outgoing)
    halo, east, west = call(
        second_columns, (sds(LEV - 1, 8, COLS), packed, packed), "second_columns_rest"
    )(adj, *edges)
    from_west, from_east = around(east, west)
    rest = call(second_rest, sds(LEV, ROWS, COLS), "second_rest", nbytes=12000000)(
        adj, halo, from_west, from_east, c_east, c_north, inc
    )

    returned = across(call(collect_kernel, plane, "collect", [acc])(back, pulled))
    edge = sds(1, 8, COLS)
    adj, *edges = call(second_pack, (sds(1, ROWS, COLS), edge, edge, edge), "second_pack")(
        residual, mask, returned
    )
    halo, east, west = call(second_columns, (sds(1, 8, COLS), packed, packed), "second_columns")(
        adj, *along(*edges)
    )
    from_west, from_east = around(east, west)
    gradient = call(second_surface, sds(LEV, ROWS, COLS), "second_surface")(
        adj, halo, from_west, from_east, c_east0, c_north0, inc, rest
    )
    linear_state = lax.dynamic_update_slice(state, linear[None], (0, 0, 0))
    return (linear_state[None], gradient[None])


def solution(mesh):
    placed = (
        P("comp", None, "lat", "lon"),
        P("comp", None, "lat", "lon"),
        P("comp", None, "lat", "lon"),
        P("lat", "lon"),
        P("comp", "lat", "lon", None, None),
        P("comp", "lat", "lon", None, None),
        P("comp", "lat", "lon", None, None),
        P("comp", "lat", "lon", None),
    )
    return jax.shard_map(
        local,
        mesh=mesh,
        in_specs=placed,
        out_specs=(P("comp", None, "lat", "lon"), P("comp", None, "lat", "lon")),
        check_vma=False,
    )
```

```python
import jax
import jax.numpy as jnp
from jax import lax
from jax.experimental import pallas as pl
from jax.experimental.pallas import tpu as pltpu
from jax.sharding import PartitionSpec as P

NSTEP = 4
HALO, WIDE = 4, 8
ROWS, COLS, LEV = 16, 512, 8
XR, XC = 24, 640
FIELDS = 2 * LEV + 1
EDGES = FIELDS + LEV // 2
SPLIT = 4
BANDS = 32
F32, BF16, I32 = jnp.float32, jnp.bfloat16, jnp.int32


def sds(*shape):
    return jax.ShapeDtypeStruct(shape, F32)


def call(kernel, out_shape, name, scratch=(), flops=100000, nbytes=1000000):
    return pl.pallas_call(
        kernel,
        out_shape=out_shape,
        scratch_shapes=list(scratch),
        name=name,
        cost_estimate=pl.CostEstimate(flops=flops, bytes_accessed=nbytes, transcendentals=0),
        compiler_params=pltpu.CompilerParams(vmem_limit_bytes=48 << 20),
    )


def tile_iota(dim):
    return lax.broadcasted_iota(I32, (8, 128), dim)


def wide_iota(width, dim):
    return lax.broadcasted_iota(I32, (8, width), dim)


def pair_edges(first, second):
    low = wide_iota(COLS, 0) < HALO
    head = jnp.where(low, first[0], pltpu.roll(second[0], HALO, 0))
    tail = jnp.where(low, pltpu.roll(first[1], HALO, 0), second[1])
    return head, tail


def put_edges(whole, paired, head_ref, tail_ref, mirror_ref):
    sub, lane = tile_iota(0), tile_iota(1)
    tiles = whole + [pair_edges(*two) for two in paired]
    for p, (head, tail) in enumerate(tiles):
        head_ref[p] = head
        tail_ref[p] = tail

    @pl.when((lax.axis_index("comp") == 1) & (lax.axis_index("lat") == BANDS - 1))
    def _():
        for p in range(len(tiles)):
            for k in range(4):
                x = tail_ref[p, :, (3 - k) * 128 : (4 - k) * 128]
                for bit in (1, 2, 4) if p < len(whole) else (1, 2):
                    x = jnp.where((sub & bit) == bit, pltpu.roll(x, bit, 0), pltpu.roll(x, 8 - bit, 0))
                mirror_ref[p, :, k * 128 : (k + 1) * 128] = jnp.take_along_axis(
                    x, 127 - lane, axis=1
                )


def taker(from_south_ref, from_north_ref, from_fold_ref):
    ocean = lax.axis_index("comp") == 1
    band = lax.axis_index("lat")
    first, last = band == 0, band == BANDS - 1
    zero = jnp.zeros((8, COLS), F32)

    def take(p):
        north = jnp.where(last, jnp.where(ocean, from_fold_ref[p], zero), from_north_ref[p])
        return north, jnp.where(first, zero, from_south_ref[p])

    return take


def split_pair(north, south):
    low = wide_iota(COLS, 0) < HALO
    return (
        jnp.where(low, north, pltpu.roll(south, HALO, 0)),
        jnp.where(low, pltpu.roll(north, HALO, 0), south),
    )


def put_columns(tiles, tile_rows, width, east_ref, west_ref, base=0):
    lane = tile_iota(1)
    for t in range(tile_rows):
        east = jnp.zeros((8, 128), F32)
        west = jnp.zeros((8, 128), F32)
        for f, tile in enumerate(tiles):
            here = (lane >= width * f) & (lane < width * (f + 1))
            x = tile(t)
            if x is None:
                continue
            first, last = x[:, 0:128], x[:, COLS - 128 : COLS]
            west = jnp.where(here, first if f == 0 else pltpu.roll(first, width * f, 1), west)
            shift = (width * f + width) % 128
            east = jnp.where(here, pltpu.roll(last, shift, 1) if shift else last, east)
        east_ref[8 * t : 8 * t + 8, base : base + 128] = east
        west_ref[8 * t : 8 * t + 8, base : base + 128] = west


def side_column(f, width, from_west, from_east):
    lane = lax.broadcasted_iota(I32, from_west.shape, 1)
    east = pltpu.roll(from_east, lax.rem(128 - width * f, 128), 1)
    west = pltpu.roll(from_west, lax.rem(256 - width - width * f, 128), 1)
    return jnp.where(lane < width, east, jnp.where(lane >= 128 - width, west, jnp.zeros_like(east)))


def narrow(x):
    low = lax.broadcasted_iota(I32, (8, x.shape[1]), 0) < HALO
    return jnp.concatenate([x[0:16], jnp.where(low, x[16:24], x[24:32])], axis=0)


def extend(main, halo, side):
    return jnp.concatenate([jnp.concatenate([main, halo], axis=0), side], axis=1)


def to_east(x):
    return pltpu.roll(x, XC - 1, 1)


def to_west(x):
    return pltpu.roll(x, 1, 1)


def to_north(x):
    return pltpu.roll(x, x.shape[0] - 1, 0)


def to_south(x):
    return pltpu.roll(x, 1, 0)


def sweep(f, c_east, c_north):
    c_west, c_south = to_west(c_east), to_south(c_north)
    for _ in range(NSTEP):
        change = c_east * (to_east(f) - f) + c_west * (to_west(f) - f)
        change = change + c_south * (to_south(f) - f)
        change = change + c_north * (to_north(f) - f)
        f = f + change
    return f


def first_pack(inc_ref, diff_ref, innov_ref, land_ref, head_ref, tail_ref, mirror_ref, mask_ref):
    ocean = lax.axis_index("comp") == 1
    mask = jnp.where(ocean, land_ref[...].astype(F32), jnp.ones((ROWS, COLS), F32))
    mask_ref[...] = mask

    def rows(ref, l):
        return ref[l, 0:8, :], ref[l, 8:16, :]

    whole = [rows(inc_ref, l) for l in range(LEV)] + [rows(diff_ref, l) for l in range(LEV)]
    whole.append((mask[0:8], mask[8:16]))
    paired = [
        (rows(innov_ref, l), rows(innov_ref, min(l + 1, LEV - 1))) for l in range(1, LEV, 2)
    ]
    put_edges(whole, paired, head_ref, tail_ref, mirror_ref)


def first_columns(
    inc_ref, diff_ref, innov_ref, mask_ref, from_south_ref, from_north_ref, from_fold_ref,
    halo_ref, innov_halo_ref, east_ref, west_ref,
):
    take = taker(from_south_ref, from_north_ref, from_fold_ref)
    for f in range(FIELDS):
        north, south = take(f)
        halo_ref[f, 0:8, :] = north
        halo_ref[f, 8:16, :] = south
    for p in range(LEV // 2):
        one, two = split_pair(*take(FIELDS + p))
        innov_halo_ref[2 * p] = one
        innov_halo_ref[2 * p + 1] = two

    def field(f):
        def tile(t):
            if t >= 2:
                return halo_ref[f, 8 * t - 16 : 8 * t - 8, :]
            rows = slice(8 * t, 8 * t + 8)
            if f < LEV:
                return inc_ref[f, rows, :]
            if f < 2 * LEV:
                return diff_ref[f - LEV, rows, :]
            return mask_ref[rows, :]

        return tile

    def innov(l):
        def tile(t):
            if t >= 2:
                return innov_halo_ref[l - 1] if t == 2 else None
            return innov_ref[l, 8 * t : 8 * t + 8, :]

        return tile

    put_columns([field(f) for f in range(16)], 4, WIDE, east_ref, west_ref)
    put_columns(
        [field(16)] + [innov(l) for l in range(1, LEV)], 4, WIDE, east_ref, west_ref, 128
    )


def start_level(l, inc_ref, diff_ref, mask_ref, halo_ref, from_west_ref, from_east_ref, shape):
    sides = from_west_ref[:, 0:128], from_east_ref[:, 0:128]
    other = from_west_ref[:, 128:256], from_east_ref[:, 128:256]
    mask = shape(extend(mask_ref[...], halo_ref[2 * LEV], side_column(0, WIDE, *other)))
    diff = shape(extend(diff_ref[l], halo_ref[LEV + l], side_column(LEV + l, WIDE, *sides)))
    f = shape(extend(inc_ref[l], halo_ref[l], side_column(l, WIDE, *sides)))
    c_east = mask * to_east(mask) * 0.5 * (diff + to_east(diff))
    c_north = mask * to_north(mask) * 0.5 * (diff + to_north(diff))
    return f, c_east, c_north


def first_surface(
    inc_ref, diff_ref, mask_ref, halo_ref, from_west_ref, from_east_ref,
    state_ref, surface_ref, c_east_ref, c_north_ref,
):
    f, c_east, c_north = start_level(
        0, inc_ref, diff_ref, mask_ref, halo_ref, from_west_ref, from_east_ref, narrow
    )
    c_east_ref[...] = c_east
    c_north_ref[...] = c_north
    f = sweep(f, c_east, c_north)[:ROWS, :COLS]
    state_ref[...] = f
    surface_ref[...] = mask_ref[...] * f


def rest_levels(low, high):
    def kernel(
        inc_ref, diff_ref, innov_ref, mask_ref, halo_ref, innov_halo_ref, from_west_ref,
        from_east_ref, *refs,
    ):
        state_ref, gradient_ref = refs[-2:]
        other = from_west_ref[0:XR, 128:256], from_east_ref[0:XR, 128:256]

        def level(l, carry):
            f, c_east, c_north = start_level(
                l, inc_ref, diff_ref, mask_ref, halo_ref, from_west_ref, from_east_ref, lambda x: x
            )
            f = narrow(sweep(f, c_east, c_north))
            state_ref[l] = f[:ROWS, :COLS]
            innov = extend(innov_ref[l], innov_halo_ref[l - 1], side_column(l, WIDE, *other))
            f = sweep(f - innov, narrow(c_east), narrow(c_north))
            gradient_ref[l] = f[:ROWS, :COLS] + inc_ref[l]
            return carry

        lax.fori_loop(low, high, level, 0)
        if len(refs) == 4:
            old_state_ref, old_gradient_ref = refs[:2]
            state_ref[1:low] = old_state_ref[1:low]
            gradient_ref[1:low] = old_gradient_ref[1:low]

    return kernel


def row_of(ref):
    return lambda h: ref[h // 4 : h // 4 + 1, (h % 4) * 128 : (h % 4) * 128 + 128]


def gather_slots(table, cells):
    high, low = lax.shift_right_logical(cells, 7), cells & 127
    found = jnp.zeros((8, 128), F32)
    for h in range(64):
        row = jnp.broadcast_to(table(h), (8, 128))
        found = jnp.where(high == h, jnp.take_along_axis(row, low, axis=1), found)
    return found


GROUP = 8
SUMS = 4


def gather_all(cells_ref, table_ref, store):
    def group(g, carry):
        for n in range(GROUP):
            b = g * GROUP + n
            store(b, gather_slots(row_of(table_ref), cells_ref[b]))
        return carry

    lax.fori_loop(0, BANDS // GROUP, group, 0)


def gather_kernel(cells_ref, table_ref, out_ref):
    def store(b, found):
        out_ref[b] = found

    gather_all(cells_ref, table_ref, store)


def scatter_band(cells, values):
    high_iota = lax.broadcasted_iota(I32, (64, 128), 0)
    low_iota = lax.broadcasted_iota(I32, (128, 128), 0)
    high, low = lax.shift_right_logical(cells, 7), cells & 127
    coarse = values.astype(BF16).astype(F32)
    fine = values - coarse
    left, right = [], []
    for k in range(8):
        at = high_iota == high[k : k + 1]
        a = jnp.where(at, coarse[k : k + 1], 0.0).astype(BF16)
        b = jnp.where(at, fine[k : k + 1], 0.0).astype(BF16)
        left.append(jnp.concatenate([a, b], axis=0))
        right.append(jnp.where(low_iota == low[k : k + 1], 1.0, 0.0).astype(BF16))
    return lax.dot_general(
        jnp.concatenate(left, axis=1),
        jnp.concatenate(right, axis=1),
        (((1,), (1,)), ((), ())),
        preferred_element_type=F32,
    )


def as_block(sums):
    return jnp.concatenate([sums.reshape(ROWS, 4, 128)[:, k, :] for k in range(4)], axis=1)


def sum_slots(cells_of, values_of, acc_ref):
    acc_ref[...] = jnp.zeros_like(acc_ref)

    def step(g, carry):
        total = acc_ref[...]
        for n in range(SUMS):
            total = total + scatter_band(cells_of(SUMS * g + n), values_of(SUMS * g + n))
        acc_ref[...] = total
        return carry

    lax.fori_loop(0, BANDS // SUMS, step, 0)
    return as_block(acc_ref[0:64, :] + acc_ref[64:128, :])


def live_of(b, weight_ref, count_ref):
    slot = tile_iota(0) * 128 + tile_iota(1)
    return jnp.where(slot < count_ref[0, b], weight_ref[b], jnp.zeros((8, 128), F32))


def couple_kernel(
    count_ref, values_ref, cells_ref, weight_ref, mask_ref, state_ref, innov_ref,
    linear_ref, residual_ref, out_ref, acc_ref, table_ref,
):
    income = sum_slots(
        lambda b: cells_ref[b], lambda b: live_of(b, weight_ref, count_ref) * values_ref[b], acc_ref
    )
    mask = mask_ref[...]
    linear = state_ref[...] + mask * income
    residual = linear - innov_ref[...]
    linear_ref[...] = linear
    residual_ref[...] = residual
    table_ref[...] = mask * residual

    def store(b, found):
        out_ref[b] = live_of(b, weight_ref, count_ref) * found

    gather_all(cells_ref, table_ref, store)


def collect_kernel(values_ref, cells_ref, out_ref, acc_ref):
    out_ref[...] = sum_slots(lambda b: cells_ref[b], lambda b: values_ref[b], acc_ref)


def second_pack(residual_ref, mask_ref, returned_ref, adj_ref, head_ref, tail_ref, mirror_ref):
    adj = residual_ref[...] + mask_ref[...] * returned_ref[...]
    adj_ref[...] = adj
    edges = adj[0:8], adj[8:16]
    put_edges([], [(edges, edges)], head_ref, tail_ref, mirror_ref)


def second_columns(
    adj_ref, from_south_ref, from_north_ref, from_fold_ref, halo_ref, east_ref, west_ref
):
    halo, _ = split_pair(*taker(from_south_ref, from_north_ref, from_fold_ref)(0))
    halo_ref[...] = halo
    put_columns(
        [lambda t: halo if t == 2 else adj_ref[8 * t : 8 * t + 8, :]], 3, HALO, east_ref, west_ref
    )


def second_surface(
    adj_ref, halo_ref, from_west_ref, from_east_ref, c_east_ref, c_north_ref, inc_ref, linear_ref,
    state_any, gradient_any, state_ref, gradient_ref,
):
    side = side_column(0, HALO, from_west_ref[...], from_east_ref[...])
    f = sweep(extend(adj_ref[...], halo_ref[...], side), c_east_ref[...], c_north_ref[...])
    gradient_ref[0] = f[:ROWS, :COLS] + inc_ref[...]
    state_ref[0] = linear_ref[...]


def across(value):
    return lax.ppermute(value, "comp", [(0, 1), (1, 0)])


def along(head, tail, mirror):
    n, m = lax.axis_size("lat"), lax.axis_size("lon")
    return (
        lax.ppermute(tail, "lat", [(i, (i + 1) % n) for i in range(n)]),
        lax.ppermute(head, "lat", [((i + 1) % n, i) for i in range(n)]),
        lax.ppermute(mirror, "lon", [(i, m - 1 - i) for i in range(m)]),
    )


def around(east, west):
    n = lax.axis_size("lon")
    return (
        lax.ppermute(east, "lon", [(i, (i + 1) % n) for i in range(n)]),
        lax.ppermute(west, "lon", [((i + 1) % n, i) for i in range(n)]),
    )


def exchange(slots):
    return lax.all_to_all(slots, "lat", 0, 0, tiled=True)


def local(
    increment, diffusivity, innovation, land_mask, pull_cells, put_cells, pull_weight, pull_count
):
    inc, diff, innov = increment[0], diffusivity[0], innovation[0]
    placed = put_cells.reshape(BANDS, 8, 128)
    weight = pull_weight.reshape(BANDS, 8, 128)
    count = pull_count.reshape(1, BANDS)
    plane = sds(ROWS, COLS)
    field = sds(LEV, ROWS, COLS)
    slots = sds(BANDS, 8, 128)
    smem = pl.BlockSpec(memory_space=pltpu.SMEM)
    vmem = pl.BlockSpec(memory_space=pltpu.VMEM)
    params = pltpu.CompilerParams(vmem_limit_bytes=48 << 20)

    edge = sds(EDGES, 8, COLS)
    *edges, mask = call(first_pack, (edge, edge, edge, plane), "first_pack")(
        inc, diff, innov, land_mask
    )
    cells, *edges = lax.optimization_barrier((pull_cells.reshape(BANDS, 8, 128), *edges))
    pulled = exchange(cells)
    packed = sds(32, 256)
    halo, innov_halo, east, west = call(
        first_columns, (sds(FIELDS, 16, COLS), sds(LEV, 8, COLS), packed, packed), "first_columns"
    )(inc, diff, innov, mask, *along(*edges))
    from_west, from_east = around(east, west)
    wide = sds(XR, XC)
    state0, surface, c_east, c_north = call(
        first_surface, (plane, plane, wide, wide), "first_surface"
    )(inc, diff, mask, halo, from_west, from_east)
    sent = call(gather_kernel, slots, "gather_slots")(pulled, across(surface))

    sent, halo = lax.optimization_barrier((sent, halo))
    values = exchange(sent)
    shared = (inc, diff, innov, mask)
    rest = call(rest_levels(1, SPLIT), (field, field), "rest_one", nbytes=10000000)(
        *shared, halo, innov_halo, from_west, from_east
    )

    values, *rest = lax.optimization_barrier((values, *rest))
    acc = pltpu.VMEM((128, 128), F32)
    linear, residual, outgoing = pl.pallas_call(
        couple_kernel,
        out_shape=(plane, plane, slots),
        in_specs=[smem] + [vmem] * 6,
        out_specs=(vmem,) * 3,
        scratch_shapes=[acc, pltpu.VMEM((ROWS, COLS), F32)],
        name="couple",
        compiler_params=params,
    )(count, values, placed, weight, mask, state0, innov[0])

    outgoing, *rest = lax.optimization_barrier((outgoing, *rest))
    back = exchange(outgoing)
    rest = pl.pallas_call(
        rest_levels(SPLIT, LEV),
        out_shape=(field, field),
        in_specs=[vmem] * 10,
        out_specs=(vmem,) * 2,
        input_output_aliases={8: 0, 9: 1},
        name="rest_two",
        cost_estimate=pl.CostEstimate(flops=100000, bytes_accessed=14000000, transcendentals=0),
        compiler_params=params,
    )(*shared, halo, innov_halo, from_west, from_east, *rest)

    back, *rest = lax.optimization_barrier((back, *rest))
    returned = across(call(collect_kernel, plane, "collect", [acc])(back, pulled))
    edge = sds(1, 8, COLS)
    adj, *edges = call(second_pack, (plane, edge, edge, edge), "second_pack")(
        residual, mask, returned
    )
    packed = sds(XR, 128)
    halo, east, west = call(second_columns, (sds(8, COLS), packed, packed), "second_columns")(
        adj, *along(*edges)
    )
    from_west, from_east = around(east, west)
    top = pl.BlockSpec((1, ROWS, COLS), lambda i: (0, 0, 0))
    whole = pl.BlockSpec(memory_space=pl.ANY)

    def full(*shape):
        return pl.BlockSpec(shape, lambda i: (0,) * len(shape))

    state, gradient = pl.pallas_call(
        second_surface,
        out_shape=(field, field),
        grid=(1,),
        in_specs=[
            full(ROWS, COLS), full(8, COLS), full(XR, 128), full(XR, 128), full(XR, XC),
            full(XR, XC), full(ROWS, COLS), full(ROWS, COLS), whole, whole,
        ],
        out_specs=(top, top),
        input_output_aliases={8: 0, 9: 1},
        name="second_surface",
        compiler_params=params,
    )(adj, halo, from_west, from_east, c_east, c_north, inc[0], linear, *rest)
    return (state[None], gradient[None])


def solution(mesh):
    placed = (
        P("comp", None, "lat", "lon"),
        P("comp", None, "lat", "lon"),
        P("comp", None, "lat", "lon"),
        P("lat", "lon"),
        P("comp", "lat", "lon", None, None),
        P("comp", "lat", "lon", None, None),
        P("comp", "lat", "lon", None, None),
        P("comp", "lat", "lon", None),
    )
    return jax.shard_map(
        local,
        mesh=mesh,
        in_specs=placed,
        out_specs=(P("comp", None, "lat", "lon"), P("comp", None, "lat", "lon")),
        check_vma=False,
    )
```

```python
import jax
import jax.numpy as jnp
from jax import lax
from jax.experimental import pallas as pl
from jax.experimental.pallas import tpu as pltpu
from jax.sharding import PartitionSpec as P

NSTEP = 4
HALO, WIDE = 4, 8
ROWS, COLS, LEV = 16, 512, 8
XR, XC = 24, 640
FIELDS = 2 * LEV + 1
EDGES = FIELDS + LEV // 2
SPLIT = 4
BANDS, CAP = 32, 1024
F32, BF16, I32 = jnp.float32, jnp.bfloat16, jnp.int32


def sds(*shape):
    return jax.ShapeDtypeStruct(shape, F32)


def call(kernel, out_shape, name, scratch=(), flops=100000, nbytes=1000000):
    return pl.pallas_call(
        kernel,
        out_shape=out_shape,
        scratch_shapes=list(scratch),
        name=name,
        cost_estimate=pl.CostEstimate(flops=flops, bytes_accessed=nbytes, transcendentals=0),
        compiler_params=pltpu.CompilerParams(vmem_limit_bytes=48 << 20),
    )


def tile_iota(dim):
    return lax.broadcasted_iota(I32, (8, 128), dim)


def wide_iota(width, dim):
    return lax.broadcasted_iota(I32, (8, width), dim)


def pair_edges(first, second):
    low = wide_iota(COLS, 0) < HALO
    head = jnp.where(low, first[0], pltpu.roll(second[0], HALO, 0))
    tail = jnp.where(low, pltpu.roll(first[1], HALO, 0), second[1])
    return head, tail


def mirror_edges(whole, tiles, tail_ref, mirror_ref):
    sub, lane = tile_iota(0), tile_iota(1)

    @pl.when((lax.axis_index("comp") == 1) & (lax.axis_index("lat") == BANDS - 1))
    def _():
        for p in range(tiles):
            for k in range(4):
                x = tail_ref[p, :, (3 - k) * 128 : (4 - k) * 128]
                for bit in (1, 2, 4) if p < whole else (1, 2):
                    x = jnp.where((sub & bit) == bit, pltpu.roll(x, bit, 0), pltpu.roll(x, 8 - bit, 0))
                mirror_ref[p, :, k * 128 : (k + 1) * 128] = jnp.take_along_axis(
                    x, 127 - lane, axis=1
                )


def taker(from_south_ref, from_north_ref, from_fold_ref):
    ocean = lax.axis_index("comp") == 1
    band = lax.axis_index("lat")
    first, last = band == 0, band == BANDS - 1
    zero = jnp.zeros((8, COLS), F32)

    def take(p):
        north = jnp.where(last, jnp.where(ocean, from_fold_ref[p], zero), from_north_ref[p])
        return north, jnp.where(first, zero, from_south_ref[p])

    return take


def split_pair(north, south):
    low = wide_iota(COLS, 0) < HALO
    return (
        jnp.where(low, north, pltpu.roll(south, HALO, 0)),
        jnp.where(low, pltpu.roll(north, HALO, 0), south),
    )


def put_columns(tiles, tile_rows, width, east_ref, west_ref, base=0):
    lane = tile_iota(1)
    for t in range(tile_rows):
        east = jnp.zeros((8, 128), F32)
        west = jnp.zeros((8, 128), F32)
        for f, tile in enumerate(tiles):
            here = (lane >= width * f) & (lane < width * (f + 1))
            x = tile(t)
            if x is None:
                continue
            first, last = x[:, 0:128], x[:, COLS - 128 : COLS]
            west = jnp.where(here, first if f == 0 else pltpu.roll(first, width * f, 1), west)
            shift = (width * f + width) % 128
            east = jnp.where(here, pltpu.roll(last, shift, 1) if shift else last, east)
        east_ref[8 * t : 8 * t + 8, base : base + 128] = east
        west_ref[8 * t : 8 * t + 8, base : base + 128] = west


def side_column(f, width, from_west, from_east):
    lane = lax.broadcasted_iota(I32, from_west.shape, 1)
    east = pltpu.roll(from_east, lax.rem(128 - width * f, 128), 1)
    west = pltpu.roll(from_west, lax.rem(256 - width - width * f, 128), 1)
    return jnp.where(lane < width, east, jnp.where(lane >= 128 - width, west, jnp.zeros_like(east)))


def narrow(x):
    low = lax.broadcasted_iota(I32, (8, x.shape[1]), 0) < HALO
    return jnp.concatenate([x[0:16], jnp.where(low, x[16:24], x[24:32])], axis=0)


def extend(main, halo, side):
    return jnp.concatenate([jnp.concatenate([main, halo], axis=0), side], axis=1)


def to_east(x):
    return pltpu.roll(x, XC - 1, 1)


def to_west(x):
    return pltpu.roll(x, 1, 1)


def to_north(x):
    return pltpu.roll(x, x.shape[0] - 1, 0)


def to_south(x):
    return pltpu.roll(x, 1, 0)


def sweep(f, c_east, c_north):
    c_west, c_south = to_west(c_east), to_south(c_north)
    for _ in range(NSTEP):
        change = c_east * (to_east(f) - f) + c_west * (to_west(f) - f)
        change = change + c_south * (to_south(f) - f)
        change = change + c_north * (to_north(f) - f)
        f = f + change
    return f


def first_pack(
    inc_hbm, diff_hbm, innov_hbm, land_hbm, head_ref, tail_ref, mirror_ref, mask_ref,
    other_mask_ref, innov_ref, land_ref, sem,
):
    copies = []

    def fetch(source, target):
        copies.append(pltpu.make_async_copy(source, target, sem.at[len(copies)]))
        copies[-1].start()

    for base, source in ((0, inc_hbm), (LEV, diff_hbm)):
        fetch(source.at[:, 0:8, :], head_ref.at[base : base + LEV])
        fetch(source.at[:, 8:16, :], tail_ref.at[base : base + LEV])
    fetch(innov_hbm.at[0:4], innov_ref.at[0:4])
    fetch(innov_hbm.at[4:8], innov_ref.at[4:8])
    fetch(land_hbm, land_ref)
    for copy in copies:
        copy.wait()

    ocean = lax.axis_index("comp") == 1
    land = land_ref[...].astype(F32)
    ones = jnp.ones((ROWS, COLS), F32)
    mask = jnp.where(ocean, land, ones)
    mask_ref[...] = mask
    other_mask_ref[...] = jnp.where(ocean, ones, land)
    head_ref[2 * LEV] = mask[0:8]
    tail_ref[2 * LEV] = mask[8:16]
    for p in range(LEV // 2):
        one, two = 2 * p + 1, min(2 * p + 2, LEV - 1)
        head, tail = pair_edges(
            (innov_ref[one, 0:8], innov_ref[one, 8:16]), (innov_ref[two, 0:8], innov_ref[two, 8:16])
        )
        head_ref[FIELDS + p] = head
        tail_ref[FIELDS + p] = tail
    mirror_edges(FIELDS, EDGES, tail_ref, mirror_ref)


def regroup(x):
    return x.reshape(8, 8, 128)


def regroup_kernel(cells_ref, out_ref):
    for g in range(BANDS // 8):
        out_ref[8 * g : 8 * g + 8] = regroup(cells_ref[8 * g : 8 * g + 8, :])


def receive_kernel(count_ref, cells_ref, weight_ref, out_ref):
    for g in range(BANDS // 8):
        rows = slice(8 * g, 8 * g + 8)
        out_ref[0, rows] = regroup(weight_ref[rows, :])
        out_ref[1, rows] = regroup(cells_ref[rows, :].astype(F32))
    slot = tile_iota(0) * 128 + tile_iota(1)
    for b in range(BANDS):
        out_ref[0, b] = jnp.where(slot < count_ref[0, b], out_ref[0, b], 0.0)


def first_columns(
    inc_ref, diff_ref, innov_ref, mask_ref, from_south_ref, from_north_ref, from_fold_ref,
    halo_ref, innov_halo_ref, east_ref, west_ref,
):
    take = taker(from_south_ref, from_north_ref, from_fold_ref)
    for f in range(FIELDS):
        north, south = take(f)
        halo_ref[f, 0:8, :] = north
        halo_ref[f, 8:16, :] = south
    for p in range(LEV // 2):
        one, two = split_pair(*take(FIELDS + p))
        innov_halo_ref[2 * p] = one
        innov_halo_ref[2 * p + 1] = two

    def field(f):
        def tile(t):
            if t >= 2:
                return halo_ref[f, 8 * t - 16 : 8 * t - 8, :]
            rows = slice(8 * t, 8 * t + 8)
            if f < LEV:
                return inc_ref[f, rows, :]
            if f < 2 * LEV:
                return diff_ref[f - LEV, rows, :]
            return mask_ref[rows, :]

        return tile

    def innov(l):
        def tile(t):
            if t >= 2:
                return innov_halo_ref[l - 1] if t == 2 else None
            return innov_ref[l, 8 * t : 8 * t + 8, :]

        return tile

    put_columns([field(f) for f in range(16)], 4, WIDE, east_ref, west_ref)
    put_columns(
        [field(16)] + [innov(l) for l in range(1, LEV)], 4, WIDE, east_ref, west_ref, 128
    )


def start_level(l, inc_ref, diff_ref, mask_ref, halo_ref, from_west_ref, from_east_ref, shape):
    sides = from_west_ref[:, 0:128], from_east_ref[:, 0:128]
    other = from_west_ref[:, 128:256], from_east_ref[:, 128:256]
    mask = shape(extend(mask_ref[...], halo_ref[2 * LEV], side_column(0, WIDE, *other)))
    diff = shape(extend(diff_ref[l], halo_ref[LEV + l], side_column(LEV + l, WIDE, *sides)))
    f = shape(extend(inc_ref[l], halo_ref[l], side_column(l, WIDE, *sides)))
    c_east = mask * to_east(mask) * 0.5 * (diff + to_east(diff))
    c_north = mask * to_north(mask) * 0.5 * (diff + to_north(diff))
    return f, c_east, c_north


def first_surface(
    inc_ref, diff_ref, innov_ref, mask_ref, halo_ref, from_west_ref, from_east_ref,
    state_ref, surface_ref, c_east_ref, c_north_ref,
):
    f, c_east, c_north = start_level(
        0, inc_ref, diff_ref, mask_ref, halo_ref, from_west_ref, from_east_ref, narrow
    )
    c_east_ref[...] = c_east
    c_north_ref[...] = c_north
    f = sweep(f, c_east, c_north)[:ROWS, :COLS]
    state_ref[0] = f
    state_ref[1] = innov_ref[0]
    surface_ref[...] = mask_ref[...] * f


def rest_levels(low, high):
    def kernel(
        inc_ref, diff_ref, innov_ref, mask_ref, halo_ref, innov_halo_ref, from_west_ref,
        from_east_ref, *refs,
    ):
        state_ref, gradient_ref = refs[-2:]
        other = from_west_ref[0:XR, 128:256], from_east_ref[0:XR, 128:256]

        def level(l, carry):
            f, c_east, c_north = start_level(
                l, inc_ref, diff_ref, mask_ref, halo_ref, from_west_ref, from_east_ref, lambda x: x
            )
            f = narrow(sweep(f, c_east, c_north))
            state_ref[l] = f[:ROWS, :COLS]
            innov = extend(innov_ref[l], innov_halo_ref[l - 1], side_column(l, WIDE, *other))
            f = sweep(f - innov, narrow(c_east), narrow(c_north))
            gradient_ref[l] = f[:ROWS, :COLS] + inc_ref[l]
            return carry

        lax.fori_loop(low, high, level, 0)
        if len(refs) == 4:
            old_state_ref, old_gradient_ref = refs[:2]
            state_ref[1:low] = old_state_ref[1:low]
            gradient_ref[1:low] = old_gradient_ref[1:low]

    return kernel


def row_of(ref):
    return lambda h: ref[h // 4 : h // 4 + 1, (h % 4) * 128 : (h % 4) * 128 + 128]


def gather_slots(table, cells):
    high, low = lax.shift_right_logical(cells, 7), cells & 127
    found = jnp.zeros((8, 128), F32)
    for h in range(64):
        row = jnp.broadcast_to(table(h), (8, 128))
        found = jnp.where(high == h, jnp.take_along_axis(row, low, axis=1), found)
    return found


GROUP = 8
SUMS = 8


def gather_all(cells_of, table_ref, store):
    def group(g, carry):
        for n in range(GROUP):
            b = g * GROUP + n
            store(b, gather_slots(row_of(table_ref), cells_of(b)))
        return carry

    lax.fori_loop(0, BANDS // GROUP, group, 0)


def gather_kernel(cells_ref, table_ref, out_ref):
    def store(b, found):
        out_ref[b] = found

    gather_all(lambda b: cells_ref[b], table_ref, store)


def scatter_band(cells, values):
    high_iota = lax.broadcasted_iota(I32, (64, 128), 0).astype(F32).astype(BF16)
    low_iota = lax.broadcasted_iota(I32, (128, 128), 0).astype(F32).astype(BF16)
    high, low = lax.shift_right_logical(cells, 7).astype(F32), (cells & 127).astype(F32)
    coarse = values.astype(BF16).astype(F32)
    fine = values - coarse
    zero, one = jnp.zeros((16, 128), BF16), jnp.ones((16, 128), BF16)
    left, right = [], []
    for k in range(8):
        h, l, a, b = (
            jnp.broadcast_to(x[k : k + 1], (16, 128)).astype(BF16) for x in (high, low, coarse, fine)
        )
        at = [high_iota[t : t + 16] == h for t in range(0, 64, 16)]
        parts = [jnp.where(here, x, zero) for x in (a, b) for here in at]
        left.append(jnp.concatenate(parts, axis=0))
        parts = [jnp.where(low_iota[t : t + 16] == l, one, zero) for t in range(0, 128, 16)]
        right.append(jnp.concatenate(parts, axis=0))
    return lax.dot_general(
        jnp.concatenate(left, axis=1),
        jnp.concatenate(right, axis=1),
        (((1,), (1,)), ((), ())),
        preferred_element_type=F32,
    )


def as_block(sums):
    return jnp.concatenate([sums.reshape(ROWS, 4, 128)[:, k, :] for k in range(4)], axis=1)


def sum_slots(cells_of, values_of, acc_ref):
    acc_ref[...] = jnp.zeros_like(acc_ref)

    def step(g, carry):
        total = acc_ref[...]
        for n in range(SUMS):
            total = total + scatter_band(cells_of(SUMS * g + n), values_of(SUMS * g + n))
        acc_ref[...] = total
        return carry

    lax.fori_loop(0, BANDS // SUMS, step, 0)
    return as_block(acc_ref[0:64, :] + acc_ref[64:128, :])


def couple_kernel(
    values_ref, slots_ref, mask_ref, state_ref, linear_ref, out_ref, acc_ref, table_ref
):
    def cells(b):
        return slots_ref[1, b].astype(I32)

    income = sum_slots(cells, lambda b: slots_ref[0, b] * values_ref[b], acc_ref)
    mask = mask_ref[...]
    linear = state_ref[0] + mask * income
    residual = linear - state_ref[1]
    linear_ref[0] = linear
    linear_ref[1] = residual
    table_ref[...] = mask * residual

    def store(b, found):
        out_ref[b] = slots_ref[0, b] * found

    gather_all(cells, table_ref, store)


def collect_kernel(values_ref, cells_ref, out_ref, acc_ref):
    out_ref[...] = sum_slots(lambda b: cells_ref[b], lambda b: values_ref[b], acc_ref)


def second_pack(linear_ref, mask_ref, returned_ref, adj_ref, head_ref, tail_ref, mirror_ref):
    adj = linear_ref[1] + mask_ref[...] * returned_ref[...]
    adj_ref[...] = adj
    head, tail = pair_edges((adj[0:8], adj[8:16]), (adj[0:8], adj[8:16]))
    head_ref[0] = head
    tail_ref[0] = tail
    mirror_edges(0, 1, tail_ref, mirror_ref)


def second_columns(
    adj_ref, from_south_ref, from_north_ref, from_fold_ref, halo_ref, east_ref, west_ref
):
    halo, _ = split_pair(*taker(from_south_ref, from_north_ref, from_fold_ref)(0))
    halo_ref[...] = halo
    put_columns(
        [lambda t: halo if t == 2 else adj_ref[8 * t : 8 * t + 8, :]], 3, HALO, east_ref, west_ref
    )


def second_surface(
    adj_ref, halo_ref, from_west_ref, from_east_ref, c_east_ref, c_north_ref, inc_ref, linear_ref,
    state_any, gradient_any, state_ref, gradient_ref,
):
    side = side_column(0, HALO, from_west_ref[...], from_east_ref[...])
    f = sweep(extend(adj_ref[...], halo_ref[...], side), c_east_ref[...], c_north_ref[...])
    gradient_ref[0] = f[:ROWS, :COLS] + inc_ref[0]
    state_ref[0] = linear_ref[0]


def across(value):
    return lax.ppermute(value, "comp", [(0, 1), (1, 0)])


def along(head, tail, mirror):
    n, m = lax.axis_size("lat"), lax.axis_size("lon")
    return (
        lax.ppermute(tail, "lat", [(i, (i + 1) % n) for i in range(n)]),
        lax.ppermute(head, "lat", [((i + 1) % n, i) for i in range(n)]),
        lax.ppermute(mirror, "lon", [(i, m - 1 - i) for i in range(m)]),
    )


def around(east, west):
    n = lax.axis_size("lon")
    return (
        lax.ppermute(east, "lon", [(i, (i + 1) % n) for i in range(n)]),
        lax.ppermute(west, "lon", [((i + 1) % n, i) for i in range(n)]),
    )


def exchange(slots):
    return lax.all_to_all(slots, "lat", 0, 0, tiled=True)


def local(
    increment, diffusivity, innovation, land_mask, pull_cells, put_cells, pull_weight, pull_count
):
    inc, diff, innov = increment[0], diffusivity[0], innovation[0]
    plane = sds(ROWS, COLS)
    pair = sds(2, ROWS, COLS)
    field = sds(LEV, ROWS, COLS)
    slots = sds(BANDS, 8, 128)
    smem = pl.BlockSpec(memory_space=pltpu.SMEM)
    vmem = pl.BlockSpec(memory_space=pltpu.VMEM)
    whole = pl.BlockSpec(memory_space=pl.ANY)
    params = pltpu.CompilerParams(vmem_limit_bytes=48 << 20)
    barrier = lax.optimization_barrier

    edge = sds(EDGES, 8, COLS)
    *edges, mask, other_mask = pl.pallas_call(
        first_pack,
        out_shape=(edge, edge, edge, plane, plane),
        in_specs=[pl.BlockSpec(memory_space=pltpu.HBM)] * 4,
        out_specs=(vmem,) * 5,
        scratch_shapes=[
            pltpu.VMEM((LEV, ROWS, COLS), F32),
            pltpu.VMEM((ROWS, COLS), I32),
            pltpu.SemaphoreType.DMA((7,)),
        ],
        name="first_pack",
        compiler_params=params,
    )(*(pltpu.with_memory_space_constraint(x, pltpu.HBM) for x in (inc, diff, innov, land_mask)))
    cells, _ = barrier((across(pull_cells.reshape(BANDS, CAP)), edges[0]))
    cells = pl.pallas_call(
        regroup_kernel, out_shape=jax.ShapeDtypeStruct(slots.shape, I32), name="regroup"
    )(cells)
    pulled = exchange(cells)
    packed = sds(32, 256)
    halo, innov_halo, east, west = call(
        first_columns, (sds(FIELDS, 16, COLS), sds(LEV, 8, COLS), packed, packed), "first_columns"
    )(inc, diff, innov, mask, *along(*edges))

    put, weight, east, west = barrier(
        (put_cells.reshape(BANDS, CAP), pull_weight.reshape(BANDS, CAP), east, west)
    )
    received = across(
        pl.pallas_call(
            receive_kernel,
            out_shape=sds(2, BANDS, 8, 128),
            in_specs=[smem, vmem, vmem],
            out_specs=vmem,
            name="receive",
            compiler_params=params,
        )(pull_count.reshape(1, BANDS), put, weight)
    )
    from_west, from_east = around(east, west)
    wide = sds(XR, XC)
    state, surface, c_east, c_north = call(
        first_surface, (pair, plane, wide, wide), "first_surface"
    )(inc, diff, innov, mask, halo, from_west, from_east)
    sent = call(gather_kernel, slots, "gather_slots")(pulled, surface)

    sent, halo, state = barrier((sent, halo, state))
    values = exchange(sent)
    state = across(state)
    shared = (inc, diff, innov, mask)
    rest = call(rest_levels(1, SPLIT), (field, field), "rest_one", nbytes=10000000)(
        *shared, halo, innov_halo, from_west, from_east
    )

    values, *rest = barrier((values, *rest))
    acc = pltpu.VMEM((128, 128), F32)
    linear, outgoing = call(
        couple_kernel, (pair, slots), "couple", [acc, pltpu.VMEM((ROWS, COLS), F32)]
    )(values, received, other_mask, state)

    outgoing, linear, *rest = barrier((outgoing, linear, *rest))
    back = exchange(outgoing)
    linear = across(linear)
    rest = pl.pallas_call(
        rest_levels(SPLIT, LEV),
        out_shape=(field, field),
        in_specs=[vmem] * 10,
        out_specs=(vmem,) * 2,
        input_output_aliases={8: 0, 9: 1},
        name="rest_two",
        cost_estimate=pl.CostEstimate(flops=100000, bytes_accessed=14000000, transcendentals=0),
        compiler_params=params,
    )(*shared, halo, innov_halo, from_west, from_east, *rest)

    back, *rest = barrier((back, *rest))
    returned = call(collect_kernel, plane, "collect", [acc])(back, pulled)
    edge = sds(1, 8, COLS)
    adj, *edges = call(second_pack, (plane, edge, edge, edge), "second_pack")(
        linear, mask, returned
    )
    packed = sds(XR, 128)
    halo, east, west = call(second_columns, (sds(8, COLS), packed, packed), "second_columns")(
        adj, *along(*edges)
    )
    from_west, from_east = around(east, west)
    top = pl.BlockSpec((1, ROWS, COLS), lambda i: (0, 0, 0))

    def full(*shape):
        return pl.BlockSpec(shape, lambda i: (0,) * len(shape))

    state, gradient = pl.pallas_call(
        second_surface,
        out_shape=(field, field),
        grid=(1,),
        in_specs=[
            full(ROWS, COLS), full(8, COLS), full(XR, 128), full(XR, 128), full(XR, XC),
            full(XR, XC), top, top, whole, whole,
        ],
        out_specs=(top, top),
        input_output_aliases={8: 0, 9: 1},
        name="second_surface",
        compiler_params=params,
    )(adj, halo, from_west, from_east, c_east, c_north, inc, linear, *rest)
    return (state[None], gradient[None])


def solution(mesh):
    placed = (
        P("comp", None, "lat", "lon"),
        P("comp", None, "lat", "lon"),
        P("comp", None, "lat", "lon"),
        P("lat", "lon"),
        P("comp", "lat", "lon", None, None),
        P("comp", "lat", "lon", None, None),
        P("comp", "lat", "lon", None, None),
        P("comp", "lat", "lon", None),
    )
    return jax.shard_map(
        local,
        mesh=mesh,
        in_specs=placed,
        out_specs=(P("comp", None, "lat", "lon"), P("comp", None, "lat", "lon")),
        check_vma=False,
    )
```

```python
import jax
import jax.numpy as jnp
from jax import lax
from jax.experimental import pallas as pl
from jax.experimental.pallas import tpu as pltpu
from jax.sharding import PartitionSpec as P

NSTEP = 4
HALO, WIDE = 4, 8
ROWS, COLS, LEV = 16, 512, 8
XR, XC = 24, 640
FIELDS = 2 * LEV + 1
EDGES = FIELDS + LEV // 2
SPLITS = 4, 8
BANDS, CAP = 32, 1024
F32, BF16, I32 = jnp.float32, jnp.bfloat16, jnp.int32


def sds(*shape):
    return jax.ShapeDtypeStruct(shape, F32)


def call(kernel, out_shape, name, scratch=(), flops=100000, nbytes=1000000):
    return pl.pallas_call(
        kernel,
        out_shape=out_shape,
        scratch_shapes=list(scratch),
        name=name,
        cost_estimate=pl.CostEstimate(flops=flops, bytes_accessed=nbytes, transcendentals=0),
        compiler_params=pltpu.CompilerParams(vmem_limit_bytes=48 << 20),
    )


def tile_iota(dim):
    return lax.broadcasted_iota(I32, (8, 128), dim)


def wide_iota(width, dim):
    return lax.broadcasted_iota(I32, (8, width), dim)


def pair_edges(first, second):
    low = wide_iota(COLS, 0) < HALO
    head = jnp.where(low, first[0], pltpu.roll(second[0], HALO, 0))
    tail = jnp.where(low, pltpu.roll(first[1], HALO, 0), second[1])
    return head, tail


def mirror_edges(whole, tiles, tail_ref, mirror_ref):
    sub, lane = tile_iota(0), tile_iota(1)

    @pl.when((lax.axis_index("comp") == 1) & (lax.axis_index("lat") == BANDS - 1))
    def _():
        for p in range(tiles):
            for k in range(4):
                x = tail_ref[p, :, (3 - k) * 128 : (4 - k) * 128]
                for bit in (1, 2, 4) if p < whole else (1, 2):
                    x = jnp.where((sub & bit) == bit, pltpu.roll(x, bit, 0), pltpu.roll(x, 8 - bit, 0))
                mirror_ref[p, :, k * 128 : (k + 1) * 128] = jnp.take_along_axis(
                    x, 127 - lane, axis=1
                )


def taker(from_south_ref, from_north_ref, from_fold_ref):
    ocean = lax.axis_index("comp") == 1
    band = lax.axis_index("lat")
    first, last = band == 0, band == BANDS - 1
    zero = jnp.zeros((8, COLS), F32)

    def take(p):
        north = jnp.where(last, jnp.where(ocean, from_fold_ref[p], zero), from_north_ref[p])
        return north, jnp.where(first, zero, from_south_ref[p])

    return take


def split_pair(north, south):
    low = wide_iota(COLS, 0) < HALO
    return (
        jnp.where(low, north, pltpu.roll(south, HALO, 0)),
        jnp.where(low, pltpu.roll(north, HALO, 0), south),
    )


def put_columns(tiles, tile_rows, width, east_ref, west_ref, base=0):
    lane = tile_iota(1)
    for t in range(tile_rows):
        east = jnp.zeros((8, 128), F32)
        west = jnp.zeros((8, 128), F32)
        for f, tile in enumerate(tiles):
            here = (lane >= width * f) & (lane < width * (f + 1))
            x = tile(t)
            if x is None:
                continue
            first, last = x[:, 0:128], x[:, COLS - 128 : COLS]
            west = jnp.where(here, first if f == 0 else pltpu.roll(first, width * f, 1), west)
            shift = (width * f + width) % 128
            east = jnp.where(here, pltpu.roll(last, shift, 1) if shift else last, east)
        east_ref[8 * t : 8 * t + 8, base : base + 128] = east
        west_ref[8 * t : 8 * t + 8, base : base + 128] = west


def side_column(f, width, from_west, from_east):
    lane = lax.broadcasted_iota(I32, from_west.shape, 1)
    east = pltpu.roll(from_east, lax.rem(128 - width * f, 128), 1)
    west = pltpu.roll(from_west, lax.rem(256 - width - width * f, 128), 1)
    return jnp.where(lane < width, east, jnp.where(lane >= 128 - width, west, jnp.zeros_like(east)))


def narrow(x):
    low = lax.broadcasted_iota(I32, (8, x.shape[1]), 0) < HALO
    return jnp.concatenate([x[0:16], jnp.where(low, x[16:24], x[24:32])], axis=0)


def extend(main, halo, side):
    return jnp.concatenate([jnp.concatenate([main, halo], axis=0), side], axis=1)


def to_east(x):
    return pltpu.roll(x, XC - 1, 1)


def to_west(x):
    return pltpu.roll(x, 1, 1)


def to_north(x):
    return pltpu.roll(x, x.shape[0] - 1, 0)


def to_south(x):
    return pltpu.roll(x, 1, 0)


def sweep(f, c_east, c_north):
    c_west, c_south = to_west(c_east), to_south(c_north)
    for _ in range(NSTEP):
        change = c_east * (to_east(f) - f) + c_west * (to_west(f) - f)
        change = change + c_south * (to_south(f) - f)
        change = change + c_north * (to_north(f) - f)
        f = f + change
    return f


def first_pack(
    inc_hbm, diff_hbm, innov_hbm, land_hbm, cells_hbm, head_ref, tail_ref, mirror_ref, mask_ref,
    other_mask_ref, slots_ref, innov_ref, land_ref, cells_ref, sem,
):
    copies = []

    def fetch(source, target):
        copies.append(pltpu.make_async_copy(source, target, sem.at[len(copies)]))
        copies[-1].start()

    fetch(cells_hbm, cells_ref)
    for base, source in ((0, inc_hbm), (LEV, diff_hbm)):
        fetch(source.at[:, 0:8, :], head_ref.at[base : base + LEV])
        fetch(source.at[:, 8:16, :], tail_ref.at[base : base + LEV])
    fetch(innov_hbm.at[0:4], innov_ref.at[0:4])
    fetch(innov_hbm.at[4:8], innov_ref.at[4:8])
    fetch(land_hbm, land_ref)
    copies[0].wait()
    for g in range(BANDS // 8):
        slots_ref[8 * g : 8 * g + 8] = regroup(cells_ref[8 * g : 8 * g + 8, :])
    for copy in copies[1:]:
        copy.wait()

    ocean = lax.axis_index("comp") == 1
    land = land_ref[...].astype(F32)
    ones = jnp.ones((ROWS, COLS), F32)
    mask = jnp.where(ocean, land, ones)
    mask_ref[...] = mask
    other_mask_ref[...] = jnp.where(ocean, ones, land)
    head_ref[2 * LEV] = mask[0:8]
    tail_ref[2 * LEV] = mask[8:16]
    for p in range(LEV // 2):
        one, two = 2 * p + 1, min(2 * p + 2, LEV - 1)
        head, tail = pair_edges(
            (innov_ref[one, 0:8], innov_ref[one, 8:16]), (innov_ref[two, 0:8], innov_ref[two, 8:16])
        )
        head_ref[FIELDS + p] = head
        tail_ref[FIELDS + p] = tail
    mirror_edges(FIELDS, EDGES, tail_ref, mirror_ref)


def regroup(x):
    return x.reshape(8, 8, 128)


def receive_kernel(count_ref, cells_ref, weight_ref, out_ref):
    for g in range(BANDS // 8):
        rows = slice(8 * g, 8 * g + 8)
        out_ref[0, rows] = regroup(weight_ref[rows, :])
        out_ref[1, rows] = regroup(cells_ref[rows, :].astype(F32))
    slot = tile_iota(0) * 128 + tile_iota(1)
    for b in range(BANDS):
        out_ref[0, b] = jnp.where(slot < count_ref[0, b], out_ref[0, b], 0.0)


def first_columns(
    inc_ref, diff_ref, innov_ref, mask_ref, from_south_ref, from_north_ref, from_fold_ref,
    halo_ref, innov_halo_ref, east_ref, west_ref,
):
    take = taker(from_south_ref, from_north_ref, from_fold_ref)
    for f in range(FIELDS):
        north, south = take(f)
        halo_ref[f, 0:8, :] = north
        halo_ref[f, 8:16, :] = south
    for p in range(LEV // 2):
        one, two = split_pair(*take(FIELDS + p))
        innov_halo_ref[2 * p] = one
        innov_halo_ref[2 * p + 1] = two

    def field(f):
        def tile(t):
            if t >= 2:
                return halo_ref[f, 8 * t - 16 : 8 * t - 8, :]
            rows = slice(8 * t, 8 * t + 8)
            if f < LEV:
                return inc_ref[f, rows, :]
            if f < 2 * LEV:
                return diff_ref[f - LEV, rows, :]
            return mask_ref[rows, :]

        return tile

    def innov(l):
        def tile(t):
            if t >= 2:
                return innov_halo_ref[l - 1] if t == 2 else None
            return innov_ref[l, 8 * t : 8 * t + 8, :]

        return tile

    put_columns([field(f) for f in range(16)], 4, WIDE, east_ref, west_ref)
    put_columns(
        [field(16)] + [innov(l) for l in range(1, LEV)], 4, WIDE, east_ref, west_ref, 128
    )


def start_level(l, inc_ref, diff_ref, mask_ref, halo_ref, from_west_ref, from_east_ref, shape):
    sides = from_west_ref[:, 0:128], from_east_ref[:, 0:128]
    other = from_west_ref[:, 128:256], from_east_ref[:, 128:256]
    mask = shape(extend(mask_ref[...], halo_ref[2 * LEV], side_column(0, WIDE, *other)))
    diff = shape(extend(diff_ref[l], halo_ref[LEV + l], side_column(LEV + l, WIDE, *sides)))
    f = shape(extend(inc_ref[l], halo_ref[l], side_column(l, WIDE, *sides)))
    c_east = mask * to_east(mask) * 0.5 * (diff + to_east(diff))
    c_north = mask * to_north(mask) * 0.5 * (diff + to_north(diff))
    return f, c_east, c_north


def first_surface(
    inc_ref, diff_ref, innov_ref, mask_ref, halo_ref, from_west_ref, from_east_ref,
    state_ref, surface_ref, c_east_ref, c_north_ref,
):
    f, c_east, c_north = start_level(
        0, inc_ref, diff_ref, mask_ref, halo_ref, from_west_ref, from_east_ref, narrow
    )
    c_east_ref[...] = c_east
    c_north_ref[...] = c_north
    f = sweep(f, c_east, c_north)[:ROWS, :COLS]
    state_ref[0] = f
    state_ref[1] = innov_ref[0]
    surface_ref[...] = mask_ref[...] * f


def rest_levels(low, high):
    def kernel(
        inc_ref, diff_ref, innov_ref, mask_ref, halo_ref, innov_halo_ref, from_west_ref,
        from_east_ref, *refs,
    ):
        state_ref, gradient_ref = refs[-2:]
        other = from_west_ref[0:XR, 128:256], from_east_ref[0:XR, 128:256]

        def level(l, carry):
            f, c_east, c_north = start_level(
                l, inc_ref, diff_ref, mask_ref, halo_ref, from_west_ref, from_east_ref, lambda x: x
            )
            f = narrow(sweep(f, c_east, c_north))
            state_ref[l] = f[:ROWS, :COLS]
            innov = extend(innov_ref[l], innov_halo_ref[l - 1], side_column(l, WIDE, *other))
            f = sweep(f - innov, narrow(c_east), narrow(c_north))
            gradient_ref[l] = f[:ROWS, :COLS] + inc_ref[l]
            return carry

        lax.fori_loop(low, high, level, 0)
        if len(refs) == 4:
            old_state_ref, old_gradient_ref = refs[:2]
            state_ref[1:low] = old_state_ref[1:low]
            gradient_ref[1:low] = old_gradient_ref[1:low]

    return kernel


def row_of(ref):
    return lambda h: ref[h // 4 : h // 4 + 1, (h % 4) * 128 : (h % 4) * 128 + 128]


def gather_slots(table, cells):
    high, low = lax.shift_right_logical(cells, 7), cells & 127
    found = jnp.zeros((8, 128), F32)
    for h in range(64):
        row = jnp.broadcast_to(table(h), (8, 128))
        found = jnp.where(high == h, jnp.take_along_axis(row, low, axis=1), found)
    return found


GROUP = 8
SUMS = 8


def gather_all(cells_of, table_ref, store):
    def group(g, carry):
        for n in range(GROUP):
            b = g * GROUP + n
            store(b, gather_slots(row_of(table_ref), cells_of(b)))
        return carry

    lax.fori_loop(0, BANDS // GROUP, group, 0)


def gather_kernel(cells_ref, table_ref, out_ref):
    def store(b, found):
        out_ref[b] = found

    gather_all(lambda b: cells_ref[b], table_ref, store)


def scatter_band(cells, values):
    high_iota = lax.broadcasted_iota(I32, (64, 128), 0).astype(F32).astype(BF16)
    low_iota = lax.broadcasted_iota(I32, (128, 128), 0).astype(F32).astype(BF16)
    high, low = lax.shift_right_logical(cells, 7).astype(F32), (cells & 127).astype(F32)
    coarse = values.astype(BF16).astype(F32)
    fine = values - coarse
    zero, one = jnp.zeros((16, 128), BF16), jnp.ones((16, 128), BF16)
    left, right = [], []
    for k in range(8):
        h, l, a, b = (
            jnp.broadcast_to(x[k : k + 1], (16, 128)).astype(BF16) for x in (high, low, coarse, fine)
        )
        at = [high_iota[t : t + 16] == h for t in range(0, 64, 16)]
        parts = [jnp.where(here, x, zero) for x in (a, b) for here in at]
        left.append(jnp.concatenate(parts, axis=0))
        parts = [jnp.where(low_iota[t : t + 16] == l, one, zero) for t in range(0, 128, 16)]
        right.append(jnp.concatenate(parts, axis=0))
    return lax.dot_general(
        jnp.concatenate(left, axis=1),
        jnp.concatenate(right, axis=1),
        (((1,), (1,)), ((), ())),
        preferred_element_type=F32,
    )


def as_block(sums):
    return jnp.concatenate([sums.reshape(ROWS, 4, 128)[:, k, :] for k in range(4)], axis=1)


def sum_slots(cells_of, values_of, acc_ref):
    acc_ref[...] = jnp.zeros_like(acc_ref)

    def step(g, carry):
        total = acc_ref[...]
        for n in range(SUMS):
            total = total + scatter_band(cells_of(SUMS * g + n), values_of(SUMS * g + n))
        acc_ref[...] = total
        return carry

    lax.fori_loop(0, BANDS // SUMS, step, 0)
    return as_block(acc_ref[0:64, :] + acc_ref[64:128, :])


def couple_kernel(
    values_ref, slots_ref, mask_ref, state_ref, linear_ref, out_ref, acc_ref, table_ref
):
    def cells(b):
        return slots_ref[1, b].astype(I32)

    income = sum_slots(cells, lambda b: slots_ref[0, b] * values_ref[b], acc_ref)
    mask = mask_ref[...]
    linear = state_ref[0] + mask * income
    residual = linear - state_ref[1]
    linear_ref[0] = linear
    linear_ref[1] = residual
    table_ref[...] = mask * residual

    def store(b, found):
        out_ref[b] = slots_ref[0, b] * found

    gather_all(cells, table_ref, store)


def collect_kernel(values_ref, cells_ref, out_ref, acc_ref):
    out_ref[...] = sum_slots(lambda b: cells_ref[b], lambda b: values_ref[b], acc_ref)


def second_pack(linear_ref, mask_ref, returned_ref, adj_ref, head_ref, tail_ref, mirror_ref):
    adj = linear_ref[1] + mask_ref[...] * returned_ref[...]
    adj_ref[...] = adj
    head, tail = pair_edges((adj[0:8], adj[8:16]), (adj[0:8], adj[8:16]))
    head_ref[0] = head
    tail_ref[0] = tail
    mirror_edges(0, 1, tail_ref, mirror_ref)


def second_columns(
    adj_ref, from_south_ref, from_north_ref, from_fold_ref, halo_ref, east_ref, west_ref
):
    halo, _ = split_pair(*taker(from_south_ref, from_north_ref, from_fold_ref)(0))
    halo_ref[...] = halo
    put_columns(
        [lambda t: halo if t == 2 else adj_ref[8 * t : 8 * t + 8, :]], 3, HALO, east_ref, west_ref
    )


def second_surface(
    adj_ref, halo_ref, from_west_ref, from_east_ref, c_east_ref, c_north_ref, inc_ref, linear_ref,
    state_any, gradient_any, state_ref, gradient_ref,
):
    side = side_column(0, HALO, from_west_ref[...], from_east_ref[...])
    f = sweep(extend(adj_ref[...], halo_ref[...], side), c_east_ref[...], c_north_ref[...])
    gradient_ref[0] = f[:ROWS, :COLS] + inc_ref[0]
    state_ref[0] = linear_ref[0]


def across(value):
    return lax.ppermute(value, "comp", [(0, 1), (1, 0)])


def along(head, tail, mirror):
    n, m = lax.axis_size("lat"), lax.axis_size("lon")
    return (
        lax.ppermute(tail, "lat", [(i, (i + 1) % n) for i in range(n)]),
        lax.ppermute(head, "lat", [((i + 1) % n, i) for i in range(n)]),
        lax.ppermute(mirror, "lon", [(i, m - 1 - i) for i in range(m)]),
    )


def around(east, west):
    n = lax.axis_size("lon")
    return (
        lax.ppermute(east, "lon", [(i, (i + 1) % n) for i in range(n)]),
        lax.ppermute(west, "lon", [((i + 1) % n, i) for i in range(n)]),
    )


def exchange(slots):
    return lax.all_to_all(slots, "lat", 0, 0, tiled=True)


def local(
    increment, diffusivity, innovation, land_mask, pull_cells, put_cells, pull_weight, pull_count
):
    inc, diff, innov = increment[0], diffusivity[0], innovation[0]
    plane = sds(ROWS, COLS)
    pair = sds(2, ROWS, COLS)
    field = sds(LEV, ROWS, COLS)
    slots = sds(BANDS, 8, 128)
    smem = pl.BlockSpec(memory_space=pltpu.SMEM)
    vmem = pl.BlockSpec(memory_space=pltpu.VMEM)
    whole = pl.BlockSpec(memory_space=pl.ANY)
    params = pltpu.CompilerParams(vmem_limit_bytes=48 << 20)
    barrier = lax.optimization_barrier

    edge = sds(EDGES, 8, COLS)
    cells = jax.ShapeDtypeStruct(slots.shape, I32)
    *edges, mask, other_mask, cells = pl.pallas_call(
        first_pack,
        out_shape=(edge, edge, edge, plane, plane, cells),
        in_specs=[pl.BlockSpec(memory_space=pltpu.HBM)] * 5,
        out_specs=(vmem,) * 6,
        scratch_shapes=[
            pltpu.VMEM((LEV, ROWS, COLS), F32),
            pltpu.VMEM((ROWS, COLS), I32),
            pltpu.VMEM((BANDS, CAP), I32),
            pltpu.SemaphoreType.DMA((8,)),
        ],
        name="first_pack",
        compiler_params=params,
    )(
        *(
            pltpu.with_memory_space_constraint(x, pltpu.HBM)
            for x in (inc, diff, innov, land_mask, pull_cells.reshape(BANDS, CAP))
        )
    )
    pulled = exchange(across(cells))
    packed = sds(32, 256)
    halo, innov_halo, east, west = call(
        first_columns, (sds(FIELDS, 16, COLS), sds(LEV, 8, COLS), packed, packed), "first_columns"
    )(inc, diff, innov, mask, *along(*edges))

    put, weight, east, west = barrier(
        (put_cells.reshape(BANDS, CAP), pull_weight.reshape(BANDS, CAP), east, west)
    )
    received = across(
        pl.pallas_call(
            receive_kernel,
            out_shape=sds(2, BANDS, 8, 128),
            in_specs=[smem, vmem, vmem],
            out_specs=vmem,
            name="receive",
            compiler_params=params,
        )(pull_count.reshape(1, BANDS), put, weight)
    )
    from_west, from_east = around(east, west)
    wide = sds(XR, XC)
    state, surface, c_east, c_north = call(
        first_surface, (pair, plane, wide, wide), "first_surface"
    )(inc, diff, innov, mask, halo, from_west, from_east)
    sent = call(gather_kernel, slots, "gather_slots")(pulled, surface)

    sent, halo, state = barrier((sent, halo, state))
    values = exchange(sent)
    state = across(state)
    shared = (inc, diff, innov, mask)
    rest = call(rest_levels(1, SPLITS[0]), (field, field), "rest_one", nbytes=10000000)(
        *shared, halo, innov_halo, from_west, from_east
    )

    values, *rest = barrier((values, *rest))
    acc = pltpu.VMEM((128, 128), F32)
    linear, outgoing = call(
        couple_kernel, (pair, slots), "couple", [acc, pltpu.VMEM((ROWS, COLS), F32)]
    )(values, received, other_mask, state)

    outgoing, linear, *rest = barrier((outgoing, linear, *rest))
    back = exchange(outgoing)
    linear = across(linear)

    def more(low, high, name, rest):
        return pl.pallas_call(
            rest_levels(low, high),
            out_shape=(field, field),
            in_specs=[vmem] * 10,
            out_specs=(vmem,) * 2,
            input_output_aliases={8: 0, 9: 1},
            name=name,
            cost_estimate=pl.CostEstimate(flops=100000, bytes_accessed=9000000, transcendentals=0),
            compiler_params=params,
        )(inc, diff, innov, mask, halo8, innov_halo, west8, east8, *rest)

    halo8, west8, east8 = halo, from_west, from_east
    rest = more(SPLITS[0], SPLITS[1], "rest_two", rest)

    back, *rest = barrier((back, *rest))
    returned = call(collect_kernel, plane, "collect", [acc])(back, pulled)
    edge = sds(1, 8, COLS)
    adj, *edges = call(second_pack, (plane, edge, edge, edge), "second_pack")(
        linear, mask, returned
    )
    packed = sds(XR, 128)
    halo, east, west = call(second_columns, (sds(8, COLS), packed, packed), "second_columns")(
        adj, *along(*edges)
    )
    from_west, from_east = around(east, west)
    top = pl.BlockSpec((1, ROWS, COLS), lambda i: (0, 0, 0))

    def full(*shape):
        return pl.BlockSpec(shape, lambda i: (0,) * len(shape))

    state, gradient = pl.pallas_call(
        second_surface,
        out_shape=(field, field),
        grid=(1,),
        in_specs=[
            full(ROWS, COLS), full(8, COLS), full(XR, 128), full(XR, 128), full(XR, XC),
            full(XR, XC), top, top, whole, whole,
        ],
        out_specs=(top, top),
        input_output_aliases={8: 0, 9: 1},
        name="second_surface",
        compiler_params=params,
    )(adj, halo, from_west, from_east, c_east, c_north, inc, linear, *rest)
    return (state[None], gradient[None])


def solution(mesh):
    placed = (
        P("comp", None, "lat", "lon"),
        P("comp", None, "lat", "lon"),
        P("comp", None, "lat", "lon"),
        P("lat", "lon"),
        P("comp", "lat", "lon", None, None),
        P("comp", "lat", "lon", None, None),
        P("comp", "lat", "lon", None, None),
        P("comp", "lat", "lon", None),
    )
    return jax.shard_map(
        local,
        mesh=mesh,
        in_specs=placed,
        out_specs=(P("comp", None, "lat", "lon"), P("comp", None, "lat", "lon")),
        check_vma=False,
    )
```

```python
import jax
import jax.numpy as jnp
from jax import lax
from jax.experimental import pallas as pl
from jax.experimental.pallas import tpu as pltpu
from jax.sharding import PartitionSpec as P

NSTEP = 4
HALO, WIDE = 4, 8
ROWS, COLS, LEV = 16, 512, 8
XR, XC = 24, 640
FIELDS = 2 * LEV + 1
EDGES = FIELDS + LEV // 2
SPLIT = 4
BANDS, CAP = 32, 1024
F32, BF16, I32 = jnp.float32, jnp.bfloat16, jnp.int32


def sds(*shape):
    return jax.ShapeDtypeStruct(shape, F32)


def call(kernel, out_shape, name, scratch=(), flops=100000, nbytes=1000000):
    return pl.pallas_call(
        kernel,
        out_shape=out_shape,
        scratch_shapes=list(scratch),
        name=name,
        cost_estimate=pl.CostEstimate(flops=flops, bytes_accessed=nbytes, transcendentals=0),
        compiler_params=pltpu.CompilerParams(vmem_limit_bytes=48 << 20),
    )


def tile_iota(dim):
    return lax.broadcasted_iota(I32, (8, 128), dim)


def wide_iota(width, dim):
    return lax.broadcasted_iota(I32, (8, width), dim)


def pair_edges(first, second):
    low = wide_iota(COLS, 0) < HALO
    head = jnp.where(low, first[0], pltpu.roll(second[0], HALO, 0))
    tail = jnp.where(low, pltpu.roll(first[1], HALO, 0), second[1])
    return head, tail


def mirror_edges(whole, tiles, tail_ref, mirror_ref):
    sub, lane = tile_iota(0), tile_iota(1)

    @pl.when((lax.axis_index("comp") == 1) & (lax.axis_index("lat") == BANDS - 1))
    def _():
        for p in range(tiles):
            for k in range(4):
                x = tail_ref[p, :, (3 - k) * 128 : (4 - k) * 128]
                for bit in (1, 2, 4) if p < whole else (1, 2):
                    x = jnp.where((sub & bit) == bit, pltpu.roll(x, bit, 0), pltpu.roll(x, 8 - bit, 0))
                mirror_ref[p, :, k * 128 : (k + 1) * 128] = jnp.take_along_axis(
                    x, 127 - lane, axis=1
                )


def taker(from_south_ref, from_north_ref, from_fold_ref):
    ocean = lax.axis_index("comp") == 1
    band = lax.axis_index("lat")
    first, last = band == 0, band == BANDS - 1
    zero = jnp.zeros((8, COLS), F32)

    def take(p):
        north = jnp.where(last, jnp.where(ocean, from_fold_ref[p], zero), from_north_ref[p])
        return north, jnp.where(first, zero, from_south_ref[p])

    return take


def split_pair(north, south):
    low = wide_iota(COLS, 0) < HALO
    return (
        jnp.where(low, north, pltpu.roll(south, HALO, 0)),
        jnp.where(low, pltpu.roll(north, HALO, 0), south),
    )


def put_columns(tiles, tile_rows, width, east_ref, west_ref, base=0):
    lane = tile_iota(1)
    for t in range(tile_rows):
        east = jnp.zeros((8, 128), F32)
        west = jnp.zeros((8, 128), F32)
        for f, tile in enumerate(tiles):
            here = (lane >= width * f) & (lane < width * (f + 1))
            x = tile(t)
            if x is None:
                continue
            first, last = x[:, 0:128], x[:, COLS - 128 : COLS]
            west = jnp.where(here, first if f == 0 else pltpu.roll(first, width * f, 1), west)
            shift = (width * f + width) % 128
            east = jnp.where(here, pltpu.roll(last, shift, 1) if shift else last, east)
        east_ref[8 * t : 8 * t + 8, base : base + 128] = east
        west_ref[8 * t : 8 * t + 8, base : base + 128] = west


def side_column(f, width, from_west, from_east):
    lane = lax.broadcasted_iota(I32, from_west.shape, 1)
    east = pltpu.roll(from_east, lax.rem(128 - width * f, 128), 1)
    west = pltpu.roll(from_west, lax.rem(256 - width - width * f, 128), 1)
    return jnp.where(lane < width, east, jnp.where(lane >= 128 - width, west, jnp.zeros_like(east)))


def narrow(x):
    low = lax.broadcasted_iota(I32, (8, x.shape[1]), 0) < HALO
    return jnp.concatenate([x[0:16], jnp.where(low, x[16:24], x[24:32])], axis=0)


def extend(main, halo, side):
    return jnp.concatenate([jnp.concatenate([main, halo], axis=0), side], axis=1)


def to_east(x):
    return pltpu.roll(x, XC - 1, 1)


def to_west(x):
    return pltpu.roll(x, 1, 1)


def to_north(x):
    return pltpu.roll(x, x.shape[0] - 1, 0)


def to_south(x):
    return pltpu.roll(x, 1, 0)


def sweep(f, c_east, c_north):
    c_west, c_south = to_west(c_east), to_south(c_north)
    for _ in range(NSTEP):
        change = c_east * (to_east(f) - f) + c_west * (to_west(f) - f)
        change = change + c_south * (to_south(f) - f)
        change = change + c_north * (to_north(f) - f)
        f = f + change
    return f


def first_pack(
    inc_hbm, diff_hbm, innov_hbm, land_hbm, cells_hbm, head_ref, tail_ref, mirror_ref, mask_ref,
    other_mask_ref, slots_ref, innov_ref, land_ref, cells_ref, sem,
):
    copies = []

    def fetch(source, target):
        copies.append(pltpu.make_async_copy(source, target, sem.at[len(copies)]))
        copies[-1].start()

    fetch(cells_hbm, cells_ref)
    for base, source in ((0, inc_hbm), (LEV, diff_hbm)):
        fetch(source.at[:, 0:8, :], head_ref.at[base : base + LEV])
        fetch(source.at[:, 8:16, :], tail_ref.at[base : base + LEV])
    fetch(innov_hbm.at[0:4], innov_ref.at[0:4])
    fetch(innov_hbm.at[4:8], innov_ref.at[4:8])
    fetch(land_hbm, land_ref)
    copies[0].wait()
    for g in range(BANDS // 8):
        slots_ref[8 * g : 8 * g + 8] = regroup(cells_ref[8 * g : 8 * g + 8, :])
    for copy in copies[1:]:
        copy.wait()

    ocean = lax.axis_index("comp") == 1
    land = land_ref[...].astype(F32)
    ones = jnp.ones((ROWS, COLS), F32)
    mask = jnp.where(ocean, land, ones)
    mask_ref[...] = mask
    other_mask_ref[...] = jnp.where(ocean, ones, land)
    head_ref[2 * LEV] = mask[0:8]
    tail_ref[2 * LEV] = mask[8:16]
    for p in range(LEV // 2):
        one, two = 2 * p + 1, min(2 * p + 2, LEV - 1)
        head, tail = pair_edges(
            (innov_ref[one, 0:8], innov_ref[one, 8:16]), (innov_ref[two, 0:8], innov_ref[two, 8:16])
        )
        head_ref[FIELDS + p] = head
        tail_ref[FIELDS + p] = tail
    mirror_edges(FIELDS, EDGES, tail_ref, mirror_ref)


def regroup(x):
    return x.reshape(8, 8, 128)


def receive_kernel(count_ref, cells_ref, weight_ref, out_ref):
    for g in range(BANDS // 8):
        rows = slice(8 * g, 8 * g + 8)
        out_ref[0, rows] = regroup(weight_ref[rows, :])
        out_ref[1, rows] = regroup(cells_ref[rows, :].astype(F32))
    slot = tile_iota(0) * 128 + tile_iota(1)
    for b in range(BANDS):
        out_ref[0, b] = jnp.where(slot < count_ref[0, b], out_ref[0, b], 0.0)


def first_columns(
    inc_ref, diff_ref, innov_ref, mask_ref, from_south_ref, from_north_ref, from_fold_ref,
    halo_ref, innov_halo_ref, east_ref, west_ref,
):
    take = taker(from_south_ref, from_north_ref, from_fold_ref)
    for f in range(FIELDS):
        north, south = take(f)
        halo_ref[f, 0:8, :] = north
        halo_ref[f, 8:16, :] = south
    for p in range(LEV // 2):
        one, two = split_pair(*take(FIELDS + p))
        innov_halo_ref[2 * p] = one
        innov_halo_ref[2 * p + 1] = two

    def field(f):
        def tile(t):
            if t >= 2:
                return halo_ref[f, 8 * t - 16 : 8 * t - 8, :]
            rows = slice(8 * t, 8 * t + 8)
            if f < LEV:
                return inc_ref[f, rows, :]
            if f < 2 * LEV:
                return diff_ref[f - LEV, rows, :]
            return mask_ref[rows, :]

        return tile

    def innov(l):
        def tile(t):
            if t >= 2:
                return innov_halo_ref[l - 1] if t == 2 else None
            return innov_ref[l, 8 * t : 8 * t + 8, :]

        return tile

    put_columns([field(f) for f in range(16)], 4, WIDE, east_ref, west_ref)
    put_columns(
        [field(16)] + [innov(l) for l in range(1, LEV)], 4, WIDE, east_ref, west_ref, 128
    )


def mask_products(mask_ref, halo_ref, from_west_ref, from_east_ref, shape):
    sides = from_west_ref[:, 128:256], from_east_ref[:, 128:256]
    mask = shape(extend(mask_ref[...], halo_ref[2 * LEV], side_column(0, WIDE, *sides)))
    return mask * to_east(mask) * 0.5, mask * to_north(mask) * 0.5


def start_level(l, masks, inc_ref, diff_ref, halo_ref, from_west_ref, from_east_ref, shape):
    sides = from_west_ref[:, 0:128], from_east_ref[:, 0:128]
    diff = shape(extend(diff_ref[l], halo_ref[LEV + l], side_column(LEV + l, WIDE, *sides)))
    f = shape(extend(inc_ref[l], halo_ref[l], side_column(l, WIDE, *sides)))
    return f, masks[0] * (diff + to_east(diff)), masks[1] * (diff + to_north(diff))


def first_surface(
    inc_ref, diff_ref, innov_ref, mask_ref, halo_ref, from_west_ref, from_east_ref,
    state_ref, surface_ref, c_east_ref, c_north_ref,
):
    masks = mask_products(mask_ref, halo_ref, from_west_ref, from_east_ref, narrow)
    f, c_east, c_north = start_level(
        0, masks, inc_ref, diff_ref, halo_ref, from_west_ref, from_east_ref, narrow
    )
    c_east_ref[...] = c_east
    c_north_ref[...] = c_north
    f = sweep(f, c_east, c_north)[:ROWS, :COLS]
    state_ref[0] = f
    state_ref[1] = innov_ref[0]
    surface_ref[...] = mask_ref[...] * f


def rest_levels(low, high):
    def kernel(
        inc_ref, diff_ref, innov_ref, mask_ref, halo_ref, innov_halo_ref, from_west_ref,
        from_east_ref, state_ref, gradient_ref, mask_east_ref, mask_north_ref,
    ):
        other = from_west_ref[0:XR, 128:256], from_east_ref[0:XR, 128:256]
        mask_east_ref[...], mask_north_ref[...] = mask_products(
            mask_ref, halo_ref, from_west_ref, from_east_ref, lambda x: x
        )

        def level(l, carry):
            masks = mask_east_ref[...], mask_north_ref[...]
            f, c_east, c_north = start_level(
                l, masks, inc_ref, diff_ref, halo_ref, from_west_ref, from_east_ref, lambda x: x
            )
            f = narrow(sweep(f, c_east, c_north))
            state_ref[l - low] = f[:ROWS, :COLS]
            innov = extend(innov_ref[l], innov_halo_ref[l - 1], side_column(l, WIDE, *other))
            f = sweep(f - innov, narrow(c_east), narrow(c_north))
            gradient_ref[l - low] = f[:ROWS, :COLS] + inc_ref[l]
            return carry

        lax.fori_loop(low, high, level, 0)

    return kernel


def row_of(ref):
    return lambda h: ref[h // 4 : h // 4 + 1, (h % 4) * 128 : (h % 4) * 128 + 128]


def gather_slots(table, cells):
    high, low = lax.shift_right_logical(cells, 7), cells & 127
    found = jnp.zeros((8, 128), F32)
    for h in range(64):
        row = jnp.broadcast_to(table(h), (8, 128))
        found = jnp.where(high == h, jnp.take_along_axis(row, low, axis=1), found)
    return found


GROUP = 8
SUMS = 16


def gather_all(cells_of, table_ref, weigh, buffer_ref, out_hbm, sem):
    def copy(g):
        rows = pl.ds(g * GROUP, GROUP)
        return pltpu.make_async_copy(buffer_ref.at[rows], out_hbm.at[rows], sem.at[g])

    def group(g, carry):
        bands = [g * GROUP + n for n in range(GROUP)]
        cells = [cells_of(b) for b in bands]
        found = [gather_slots(row_of(table_ref), at) for at in cells]
        for b, x in zip(bands, found):
            buffer_ref[b] = weigh(b, x)
        copy(g).start()
        return carry

    lax.fori_loop(0, BANDS // GROUP, group, 0)
    for g in range(BANDS // GROUP):
        copy(g).wait()


def gather_kernel(cells_ref, table_ref, out_hbm, buffer_ref, sem):
    gather_all(
        lambda b: cells_ref[b], table_ref, lambda b, found: found, buffer_ref, out_hbm, sem
    )


def scatter_band(cells, values):
    high_iota = lax.broadcasted_iota(I32, (64, 128), 0).astype(F32).astype(BF16)
    low_iota = lax.broadcasted_iota(I32, (128, 128), 0).astype(F32).astype(BF16)
    high, low = lax.shift_right_logical(cells, 7).astype(F32), (cells & 127).astype(F32)
    coarse = values.astype(BF16).astype(F32)
    fine = values - coarse
    zero, one = jnp.zeros((16, 128), BF16), jnp.ones((16, 128), BF16)
    left, right = [], []
    for k in range(8):
        h, l, a, b = (
            jnp.broadcast_to(x[k : k + 1], (16, 128)).astype(BF16) for x in (high, low, coarse, fine)
        )
        at = [high_iota[t : t + 16] == h for t in range(0, 64, 16)]
        parts = [jnp.where(here, x, zero) for x in (a, b) for here in at]
        left.append(jnp.concatenate(parts, axis=0))
        parts = [jnp.where(low_iota[t : t + 16] == l, one, zero) for t in range(0, 128, 16)]
        right.append(jnp.concatenate(parts, axis=0))
    return lax.dot_general(
        jnp.concatenate(left, axis=1),
        jnp.concatenate(right, axis=1),
        (((1,), (1,)), ((), ())),
        preferred_element_type=F32,
    )


def as_block(sums):
    return jnp.concatenate([sums.reshape(ROWS, 4, 128)[:, k, :] for k in range(4)], axis=1)


def sum_slots(cells_of, values_of, acc_ref):
    acc_ref[...] = jnp.zeros_like(acc_ref)

    def step(g, carry):
        total = acc_ref[...]
        for n in range(SUMS):
            total = total + scatter_band(cells_of(SUMS * g + n), values_of(SUMS * g + n))
        acc_ref[...] = total
        return carry

    lax.fori_loop(0, BANDS // SUMS, step, 0)
    return as_block(acc_ref[0:64, :] + acc_ref[64:128, :])


def couple_kernel(
    values_ref, slots_ref, mask_ref, state_ref, linear_ref, out_hbm, acc_ref, table_ref,
    buffer_ref, sem,
):
    def cells(b):
        return slots_ref[1, b].astype(I32)

    income = sum_slots(cells, lambda b: slots_ref[0, b] * values_ref[b], acc_ref)
    mask = mask_ref[...]
    linear = state_ref[0] + mask * income
    residual = linear - state_ref[1]
    linear_ref[0] = linear
    linear_ref[1] = residual
    table_ref[...] = mask * residual

    gather_all(
        cells, table_ref, lambda b, found: slots_ref[0, b] * found, buffer_ref, out_hbm, sem
    )


def collect_kernel(values_ref, cells_ref, out_ref, acc_ref):
    out_ref[...] = sum_slots(lambda b: cells_ref[b], lambda b: values_ref[b], acc_ref)


def second_pack(linear_ref, mask_ref, returned_ref, adj_ref, head_ref, tail_ref, mirror_ref):
    adj = linear_ref[1] + mask_ref[...] * returned_ref[...]
    adj_ref[...] = adj
    head, tail = pair_edges((adj[0:8], adj[8:16]), (adj[0:8], adj[8:16]))
    head_ref[0] = head
    tail_ref[0] = tail
    mirror_edges(0, 1, tail_ref, mirror_ref)


def second_columns(
    adj_ref, from_fold_ref, from_south_ref, from_north_ref, halo_ref, east_ref, west_ref
):
    halo, _ = split_pair(*taker(from_south_ref, from_north_ref, from_fold_ref)(0))
    halo_ref[...] = halo
    put_columns(
        [lambda t: halo if t == 2 else adj_ref[8 * t : 8 * t + 8, :]], 3, HALO, east_ref, west_ref
    )


def second_surface(
    adj_ref, halo_ref, from_west_ref, from_east_ref, c_east_ref, c_north_ref, inc_ref, linear_ref,
    state_one, gradient_one, state_two, gradient_two, state_hbm, gradient_hbm, top_ref, sem,
):
    copies = []

    def store(source, target):
        copies.append(pltpu.make_async_copy(source, target, sem.at[len(copies)]))
        copies[-1].start()

    store(linear_ref.at[0:1], state_hbm.at[0:1])
    store(state_one, state_hbm.at[1:SPLIT])
    store(gradient_one, gradient_hbm.at[1:SPLIT])
    store(state_two, state_hbm.at[SPLIT:LEV])
    store(gradient_two, gradient_hbm.at[SPLIT:LEV])
    side = side_column(0, HALO, from_west_ref[...], from_east_ref[...])
    f = sweep(extend(adj_ref[...], halo_ref[...], side), c_east_ref[...], c_north_ref[...])
    top_ref[0] = f[:ROWS, :COLS] + inc_ref[...]
    store(top_ref, gradient_hbm.at[0:1])
    for copy in copies:
        copy.wait()


def across(value):
    return lax.ppermute(value, "comp", [(0, 1), (1, 0)])


def along(head, tail, mirror):
    n, m = lax.axis_size("lat"), lax.axis_size("lon")
    return (
        lax.ppermute(tail, "lat", [(i, (i + 1) % n) for i in range(n)]),
        lax.ppermute(head, "lat", [((i + 1) % n, i) for i in range(n)]),
        lax.ppermute(mirror, "lon", [(i, m - 1 - i) for i in range(m)]),
    )


def around(east, west):
    n = lax.axis_size("lon")
    return (
        lax.ppermute(east, "lon", [(i, (i + 1) % n) for i in range(n)]),
        lax.ppermute(west, "lon", [((i + 1) % n, i) for i in range(n)]),
    )


def exchange(slots):
    return lax.all_to_all(slots, "lat", 0, 0, tiled=True)


def local(
    increment, diffusivity, innovation, land_mask, pull_cells, put_cells, pull_weight, pull_count
):
    inc, diff, innov = increment[0], diffusivity[0], innovation[0]
    plane = sds(ROWS, COLS)
    pair = sds(2, ROWS, COLS)
    field = sds(LEV, ROWS, COLS)
    slots = sds(BANDS, 8, 128)
    smem = pl.BlockSpec(memory_space=pltpu.SMEM)
    vmem = pl.BlockSpec(memory_space=pltpu.VMEM)
    params = pltpu.CompilerParams(vmem_limit_bytes=48 << 20)
    barrier = lax.optimization_barrier

    edge = sds(EDGES, 8, COLS)
    cells = jax.ShapeDtypeStruct(slots.shape, I32)
    *edges, mask, other_mask, cells = pl.pallas_call(
        first_pack,
        out_shape=(edge, edge, edge, plane, plane, cells),
        in_specs=[pl.BlockSpec(memory_space=pltpu.HBM)] * 5,
        out_specs=(vmem,) * 6,
        scratch_shapes=[
            pltpu.VMEM((LEV, ROWS, COLS), F32),
            pltpu.VMEM((ROWS, COLS), I32),
            pltpu.VMEM((BANDS, CAP), I32),
            pltpu.SemaphoreType.DMA((8,)),
        ],
        name="first_pack",
        compiler_params=params,
    )(
        *(
            pltpu.with_memory_space_constraint(x, pltpu.HBM)
            for x in (inc, diff, innov, land_mask, pull_cells.reshape(BANDS, CAP))
        )
    )
    pulled = exchange(across(cells))
    packed = sds(32, 256)
    halo, innov_halo, east, west = call(
        first_columns, (sds(FIELDS, 16, COLS), sds(LEV, 8, COLS), packed, packed), "first_columns"
    )(inc, diff, innov, mask, *along(*edges))

    put, weight, east, west = barrier(
        (put_cells.reshape(BANDS, CAP), pull_weight.reshape(BANDS, CAP), east, west)
    )
    received = across(
        pl.pallas_call(
            receive_kernel,
            out_shape=sds(2, BANDS, 8, 128),
            in_specs=[smem, vmem, vmem],
            out_specs=vmem,
            name="receive",
            compiler_params=params,
        )(pull_count.reshape(1, BANDS), put, weight)
    )
    from_west, from_east = around(east, west)
    wide = sds(XR, XC)
    state, surface, c_east, c_north = call(
        first_surface, (pair, plane, wide, wide), "first_surface"
    )(inc, diff, innov, mask, halo, from_west, from_east)
    hbm = pl.BlockSpec(memory_space=pltpu.HBM)
    groups = [pltpu.VMEM((BANDS, 8, 128), F32), pltpu.SemaphoreType.DMA((BANDS // GROUP,))]
    sent = pl.pallas_call(
        gather_kernel,
        out_shape=slots,
        in_specs=[vmem] * 2,
        out_specs=hbm,
        scratch_shapes=groups,
        name="gather_slots",
        compiler_params=params,
    )(pulled, surface)

    sent, halo, state = barrier((sent, halo, state))
    values = exchange(sent)
    state = across(state)
    halo8, west8, east8 = halo, from_west, from_east

    def levels(low, high, name):
        some = sds(high - low, ROWS, COLS)
        wide8 = pltpu.VMEM((32, XC), F32)
        return call(rest_levels(low, high), (some, some), name, [wide8, wide8], nbytes=12000000)

    rest_one = levels(1, SPLIT, "rest_one")(
        inc, diff, innov, mask, halo8, innov_halo, west8, east8
    )

    values, *rest_one = barrier((values, *rest_one))
    acc = pltpu.VMEM((128, 128), F32)
    linear, outgoing = pl.pallas_call(
        couple_kernel,
        out_shape=(pair, slots),
        in_specs=[vmem] * 4,
        out_specs=(vmem, hbm),
        scratch_shapes=[acc, pltpu.VMEM((ROWS, COLS), F32), *groups],
        name="couple",
        compiler_params=params,
    )(values, received, other_mask, state)

    outgoing, linear, halo8 = barrier((outgoing, linear, halo8))
    back = exchange(outgoing)
    linear = across(linear)
    rest_two = levels(SPLIT, LEV, "rest_two")(
        inc, diff, innov, mask, halo8, innov_halo, west8, east8
    )

    back, *rest_two = barrier((back, *rest_two))
    returned = call(collect_kernel, plane, "collect", [acc])(back, pulled)
    edge = sds(1, 8, COLS)
    adj, *edges = call(second_pack, (plane, edge, edge, edge), "second_pack")(
        linear, mask, returned
    )
    packed = sds(XR, 128)
    south, north, fold = along(*edges)
    halo, east, west = call(second_columns, (sds(8, COLS), packed, packed), "second_columns")(
        adj, fold, south, north
    )
    from_west, from_east = around(east, west)
    state, gradient = pl.pallas_call(
        second_surface,
        out_shape=(field, field),
        in_specs=[vmem] * 12,
        out_specs=(hbm, hbm),
        scratch_shapes=[pltpu.VMEM((1, ROWS, COLS), F32), pltpu.SemaphoreType.DMA((6,))],
        name="second_surface",
        compiler_params=params,
    )(
        adj, halo, from_west, from_east, c_east, c_north, inc[0], linear, *rest_one, *rest_two
    )
    return (state[None], gradient[None])


def solution(mesh):
    placed = (
        P("comp", None, "lat", "lon"),
        P("comp", None, "lat", "lon"),
        P("comp", None, "lat", "lon"),
        P("lat", "lon"),
        P("comp", "lat", "lon", None, None),
        P("comp", "lat", "lon", None, None),
        P("comp", "lat", "lon", None, None),
        P("comp", "lat", "lon", None),
    )
    return jax.shard_map(
        local,
        mesh=mesh,
        in_specs=placed,
        out_specs=(P("comp", None, "lat", "lon"), P("comp", None, "lat", "lon")),
        check_vma=False,
    )
```

```python
import jax
import jax.numpy as jnp
from jax import lax
from jax.experimental import pallas as pl
from jax.experimental.pallas import tpu as pltpu
from jax.sharding import PartitionSpec as P

NSTEP = 4
HALO, WIDE = 4, 8
ROWS, COLS, LEV = 16, 512, 8
XR, XC = 24, 640
FIELDS = 2 * LEV + 1
EDGES = FIELDS + LEV // 2
SPLIT = 5
BANDS, CAP = 32, 1024
F32, BF16, I32 = jnp.float32, jnp.bfloat16, jnp.int32


def sds(*shape):
    return jax.ShapeDtypeStruct(shape, F32)


def call(kernel, out_shape, name, scratch=(), flops=100000, nbytes=1000000):
    return pl.pallas_call(
        kernel,
        out_shape=out_shape,
        scratch_shapes=list(scratch),
        name=name,
        cost_estimate=pl.CostEstimate(flops=flops, bytes_accessed=nbytes, transcendentals=0),
        compiler_params=pltpu.CompilerParams(vmem_limit_bytes=48 << 20),
    )


def tile_iota(dim):
    return lax.broadcasted_iota(I32, (8, 128), dim)


def wide_iota(width, dim):
    return lax.broadcasted_iota(I32, (8, width), dim)


def pair_edges(first, second):
    low = wide_iota(COLS, 0) < HALO
    head = jnp.where(low, first[0], pltpu.roll(second[0], HALO, 0))
    tail = jnp.where(low, pltpu.roll(first[1], HALO, 0), second[1])
    return head, tail


def mirror_edges(whole, tiles, tail_ref, mirror_ref):
    sub, lane = tile_iota(0), tile_iota(1)

    @pl.when((lax.axis_index("comp") == 1) & (lax.axis_index("lat") == BANDS - 1))
    def _():
        for p in range(tiles):
            for k in range(4):
                x = tail_ref[p, :, (3 - k) * 128 : (4 - k) * 128]
                for bit in (1, 2, 4) if p < whole else (1, 2):
                    x = jnp.where((sub & bit) == bit, pltpu.roll(x, bit, 0), pltpu.roll(x, 8 - bit, 0))
                mirror_ref[p, :, k * 128 : (k + 1) * 128] = jnp.take_along_axis(
                    x, 127 - lane, axis=1
                )


def taker(from_south_ref, from_north_ref, from_fold_ref):
    ocean = lax.axis_index("comp") == 1
    band = lax.axis_index("lat")
    first, last = band == 0, band == BANDS - 1
    zero = jnp.zeros((8, COLS), F32)

    def take(p):
        north = jnp.where(last, jnp.where(ocean, from_fold_ref[p], zero), from_north_ref[p])
        return north, jnp.where(first, zero, from_south_ref[p])

    return take


def split_pair(north, south):
    low = wide_iota(COLS, 0) < HALO
    return (
        jnp.where(low, north, pltpu.roll(south, HALO, 0)),
        jnp.where(low, pltpu.roll(north, HALO, 0), south),
    )


def put_columns(tiles, tile_rows, width, east_ref, west_ref, base=0):
    lane = tile_iota(1)
    for t in range(tile_rows):
        east = jnp.zeros((8, 128), F32)
        west = jnp.zeros((8, 128), F32)
        for f, tile in enumerate(tiles):
            here = (lane >= width * f) & (lane < width * (f + 1))
            x = tile(t)
            if x is None:
                continue
            first, last = x[:, 0:128], x[:, COLS - 128 : COLS]
            west = jnp.where(here, first if f == 0 else pltpu.roll(first, width * f, 1), west)
            shift = (width * f + width) % 128
            east = jnp.where(here, pltpu.roll(last, shift, 1) if shift else last, east)
        east_ref[8 * t : 8 * t + 8, base : base + 128] = east
        west_ref[8 * t : 8 * t + 8, base : base + 128] = west


def side_column(f, width, from_west, from_east):
    lane = lax.broadcasted_iota(I32, from_west.shape, 1)
    east = pltpu.roll(from_east, lax.rem(128 - width * f, 128), 1)
    west = pltpu.roll(from_west, lax.rem(256 - width - width * f, 128), 1)
    return jnp.where(lane < width, east, jnp.where(lane >= 128 - width, west, jnp.zeros_like(east)))


def narrow(x):
    low = lax.broadcasted_iota(I32, (8, x.shape[1]), 0) < HALO
    return jnp.concatenate([x[0:16], jnp.where(low, x[16:24], x[24:32])], axis=0)


def extend(main, halo, side):
    return jnp.concatenate([jnp.concatenate([main, halo], axis=0), side], axis=1)


def to_east(x):
    return pltpu.roll(x, XC - 1, 1)


def to_west(x):
    return pltpu.roll(x, 1, 1)


def to_north(x):
    return pltpu.roll(x, x.shape[0] - 1, 0)


def to_south(x):
    return pltpu.roll(x, 1, 0)


def sweep(f, c_east, c_north):
    c_west, c_south = to_west(c_east), to_south(c_north)
    for _ in range(NSTEP):
        change = c_east * (to_east(f) - f) + c_west * (to_west(f) - f)
        change = change + c_south * (to_south(f) - f)
        change = change + c_north * (to_north(f) - f)
        f = f + change
    return f


def first_pack(
    inc_hbm, diff_hbm, innov_hbm, land_hbm, cells_hbm, head_ref, tail_ref, mirror_ref, mask_ref,
    other_mask_ref, slots_ref, innov_ref, land_ref, cells_ref, sem,
):
    copies = []

    def fetch(source, target):
        copies.append(pltpu.make_async_copy(source, target, sem.at[len(copies)]))
        copies[-1].start()

    fetch(cells_hbm, cells_ref)
    for base, source in ((0, inc_hbm), (LEV, diff_hbm)):
        fetch(source.at[:, 0:8, :], head_ref.at[base : base + LEV])
        fetch(source.at[:, 8:16, :], tail_ref.at[base : base + LEV])
    fetch(innov_hbm.at[0:4], innov_ref.at[0:4])
    fetch(innov_hbm.at[4:8], innov_ref.at[4:8])
    fetch(land_hbm, land_ref)
    copies[0].wait()
    for g in range(BANDS // 8):
        slots_ref[8 * g : 8 * g + 8] = regroup(cells_ref[8 * g : 8 * g + 8, :])
    for copy in copies[1:]:
        copy.wait()

    ocean = lax.axis_index("comp") == 1
    land = land_ref[...].astype(F32)
    ones = jnp.ones((ROWS, COLS), F32)
    mask = jnp.where(ocean, land, ones)
    mask_ref[...] = mask
    other_mask_ref[...] = jnp.where(ocean, ones, land)
    head_ref[2 * LEV] = mask[0:8]
    tail_ref[2 * LEV] = mask[8:16]
    for p in range(LEV // 2):
        one, two = 2 * p + 1, min(2 * p + 2, LEV - 1)
        head, tail = pair_edges(
            (innov_ref[one, 0:8], innov_ref[one, 8:16]), (innov_ref[two, 0:8], innov_ref[two, 8:16])
        )
        head_ref[FIELDS + p] = head
        tail_ref[FIELDS + p] = tail
    mirror_edges(FIELDS, EDGES, tail_ref, mirror_ref)


def regroup(x):
    return x.reshape(8, 8, 128)


def receive_kernel(count_ref, cells_ref, weight_ref, out_ref):
    for g in range(BANDS // 8):
        rows = slice(8 * g, 8 * g + 8)
        out_ref[0, rows] = regroup(weight_ref[rows, :])
        out_ref[1, rows] = regroup(cells_ref[rows, :].astype(F32))
    slot = tile_iota(0) * 128 + tile_iota(1)
    for b in range(BANDS):
        out_ref[0, b] = jnp.where(slot < count_ref[0, b], out_ref[0, b], 0.0)


def first_columns(
    inc_ref, diff_ref, innov_ref, mask_ref, from_south_ref, from_north_ref, from_fold_ref,
    halo_ref, innov_halo_ref, east_ref, west_ref,
):
    take = taker(from_south_ref, from_north_ref, from_fold_ref)
    for f in range(FIELDS):
        north, south = take(f)
        halo_ref[f, 0:8, :] = north
        halo_ref[f, 8:16, :] = south
    for p in range(LEV // 2):
        one, two = split_pair(*take(FIELDS + p))
        innov_halo_ref[2 * p] = one
        innov_halo_ref[2 * p + 1] = two

    def field(f):
        def tile(t):
            if t >= 2:
                return halo_ref[f, 8 * t - 16 : 8 * t - 8, :]
            rows = slice(8 * t, 8 * t + 8)
            if f < LEV:
                return inc_ref[f, rows, :]
            if f < 2 * LEV:
                return diff_ref[f - LEV, rows, :]
            return mask_ref[rows, :]

        return tile

    def innov(l):
        def tile(t):
            if t >= 2:
                return innov_halo_ref[l - 1] if t == 2 else None
            return innov_ref[l, 8 * t : 8 * t + 8, :]

        return tile

    put_columns([field(f) for f in range(16)], 4, WIDE, east_ref, west_ref)
    put_columns(
        [field(16)] + [innov(l) for l in range(1, LEV)], 4, WIDE, east_ref, west_ref, 128
    )


def mask_products(mask_ref, halo_ref, from_west_ref, from_east_ref, shape):
    sides = from_west_ref[:, 128:256], from_east_ref[:, 128:256]
    mask = shape(extend(mask_ref[...], halo_ref[2 * LEV], side_column(0, WIDE, *sides)))
    return mask * to_east(mask) * 0.5, mask * to_north(mask) * 0.5


def start_level(l, masks, inc_ref, diff_ref, halo_ref, from_west_ref, from_east_ref, shape):
    sides = from_west_ref[:, 0:128], from_east_ref[:, 0:128]
    diff = shape(extend(diff_ref[l], halo_ref[LEV + l], side_column(LEV + l, WIDE, *sides)))
    f = shape(extend(inc_ref[l], halo_ref[l], side_column(l, WIDE, *sides)))
    return f, masks[0] * (diff + to_east(diff)), masks[1] * (diff + to_north(diff))


def first_surface(
    inc_ref, diff_ref, innov_ref, mask_ref, halo_ref, from_west_ref, from_east_ref,
    state_ref, surface_ref, c_east_ref, c_north_ref,
):
    masks = mask_products(mask_ref, halo_ref, from_west_ref, from_east_ref, narrow)
    f, c_east, c_north = start_level(
        0, masks, inc_ref, diff_ref, halo_ref, from_west_ref, from_east_ref, narrow
    )
    c_east_ref[...] = c_east
    c_north_ref[...] = c_north
    f = sweep(f, c_east, c_north)[:ROWS, :COLS]
    state_ref[0] = f
    state_ref[1] = innov_ref[0]
    surface_ref[...] = mask_ref[...] * f


def rest_levels(low, high):
    def kernel(
        inc_ref, diff_ref, innov_ref, mask_ref, halo_ref, innov_halo_ref, from_west_ref,
        from_east_ref, state_ref, gradient_ref, mask_east_ref, mask_north_ref,
    ):
        other = from_west_ref[0:XR, 128:256], from_east_ref[0:XR, 128:256]
        mask_east_ref[...], mask_north_ref[...] = mask_products(
            mask_ref, halo_ref, from_west_ref, from_east_ref, lambda x: x
        )

        def level(l, carry):
            masks = mask_east_ref[...], mask_north_ref[...]
            f, c_east, c_north = start_level(
                l, masks, inc_ref, diff_ref, halo_ref, from_west_ref, from_east_ref, lambda x: x
            )
            f = narrow(sweep(f, c_east, c_north))
            state_ref[l - low] = f[:ROWS, :COLS]
            innov = extend(innov_ref[l], innov_halo_ref[l - 1], side_column(l, WIDE, *other))
            f = sweep(f - innov, narrow(c_east), narrow(c_north))
            gradient_ref[l - low] = f[:ROWS, :COLS] + inc_ref[l]
            return carry

        lax.fori_loop(low, high, level, 0)

    return kernel


def row_of(ref):
    return lambda h: ref[h // 4 : h // 4 + 1, (h % 4) * 128 : (h % 4) * 128 + 128]


def gather_slots(table, cells):
    high, low = lax.shift_right_logical(cells, 7), cells & 127
    found = jnp.zeros((8, 128), F32)
    for h in range(64):
        row = jnp.broadcast_to(table(h), (8, 128))
        found = jnp.where(high == h, jnp.take_along_axis(row, low, axis=1), found)
    return found


GROUP = 8
SUMS = 16


def gather_all(cells_of, table_ref, weigh, buffer_ref, out_hbm, sem):
    def copy(g):
        rows = pl.ds(g * GROUP, GROUP)
        return pltpu.make_async_copy(buffer_ref.at[rows], out_hbm.at[rows], sem.at[g])

    def group(g, carry):
        bands = [g * GROUP + n for n in range(GROUP)]
        cells = [cells_of(b) for b in bands]
        found = [gather_slots(row_of(table_ref), at) for at in cells]
        for b, x in zip(bands, found):
            buffer_ref[b] = weigh(b, x)
        copy(g).start()
        return carry

    lax.fori_loop(0, BANDS // GROUP, group, 0)
    for g in range(BANDS // GROUP):
        copy(g).wait()


def gather_kernel(cells_ref, table_ref, out_hbm, buffer_ref, sem):
    gather_all(
        lambda b: cells_ref[b], table_ref, lambda b, found: found, buffer_ref, out_hbm, sem
    )


def scatter_band(cells, values):
    high_iota = lax.broadcasted_iota(I32, (64, 128), 0).astype(F32).astype(BF16)
    low_iota = lax.broadcasted_iota(I32, (128, 128), 0).astype(F32).astype(BF16)
    high, low = lax.shift_right_logical(cells, 7).astype(F32), (cells & 127).astype(F32)
    coarse = values.astype(BF16).astype(F32)
    fine = values - coarse
    zero, one = jnp.zeros((16, 128), BF16), jnp.ones((16, 128), BF16)
    left, right = [], []
    for k in range(8):
        h, l, a, b = (
            jnp.broadcast_to(x[k : k + 1], (16, 128)).astype(BF16) for x in (high, low, coarse, fine)
        )
        at = [high_iota[t : t + 16] == h for t in range(0, 64, 16)]
        parts = [jnp.where(here, x, zero) for x in (a, b) for here in at]
        left.append(jnp.concatenate(parts, axis=0))
        parts = [jnp.where(low_iota[t : t + 16] == l, one, zero) for t in range(0, 128, 16)]
        right.append(jnp.concatenate(parts, axis=0))
    return lax.dot_general(
        jnp.concatenate(left, axis=1),
        jnp.concatenate(right, axis=1),
        (((1,), (1,)), ((), ())),
        preferred_element_type=F32,
    )


def as_block(sums):
    return jnp.concatenate([sums.reshape(ROWS, 4, 128)[:, k, :] for k in range(4)], axis=1)


def sum_slots(cells_of, values_of, acc_ref):
    acc_ref[...] = jnp.zeros_like(acc_ref)

    def step(g, carry):
        total = acc_ref[...]
        for n in range(SUMS):
            total = total + scatter_band(cells_of(SUMS * g + n), values_of(SUMS * g + n))
        acc_ref[...] = total
        return carry

    lax.fori_loop(0, BANDS // SUMS, step, 0)
    return as_block(acc_ref[0:64, :] + acc_ref[64:128, :])


def couple_kernel(
    values_ref, slots_ref, mask_ref, state_ref, linear_ref, out_hbm, acc_ref, table_ref,
    buffer_ref, sem,
):
    def cells(b):
        return slots_ref[1, b].astype(I32)

    income = sum_slots(cells, lambda b: slots_ref[0, b] * values_ref[b], acc_ref)
    mask = mask_ref[...]
    linear = state_ref[0] + mask * income
    residual = linear - state_ref[1]
    linear_ref[0] = linear
    linear_ref[1] = residual
    table_ref[...] = mask * residual

    gather_all(
        cells, table_ref, lambda b, found: slots_ref[0, b] * found, buffer_ref, out_hbm, sem
    )


def collect_kernel(values_ref, cells_ref, out_ref, acc_ref):
    out_ref[...] = sum_slots(lambda b: cells_ref[b], lambda b: values_ref[b], acc_ref)


def second_pack(linear_ref, mask_ref, returned_ref, adj_ref, head_ref, tail_ref, mirror_ref):
    adj = linear_ref[1] + mask_ref[...] * returned_ref[...]
    adj_ref[...] = adj
    head, tail = pair_edges((adj[0:8], adj[8:16]), (adj[0:8], adj[8:16]))
    head_ref[0] = head
    tail_ref[0] = tail
    mirror_edges(0, 1, tail_ref, mirror_ref)


def second_columns(
    adj_ref, from_fold_ref, from_south_ref, from_north_ref, halo_ref, east_ref, west_ref
):
    halo, _ = split_pair(*taker(from_south_ref, from_north_ref, from_fold_ref)(0))
    halo_ref[...] = halo
    put_columns(
        [lambda t: halo if t == 2 else adj_ref[8 * t : 8 * t + 8, :]], 3, HALO, east_ref, west_ref
    )


def second_surface(
    adj_ref, halo_ref, from_west_ref, from_east_ref, c_east_ref, c_north_ref, inc_ref, linear_ref,
    state_one, gradient_one, state_two, gradient_two, state_hbm, gradient_hbm, top_ref, sem,
):
    copies = []

    def store(source, target):
        copies.append(pltpu.make_async_copy(source, target, sem.at[len(copies)]))
        copies[-1].start()

    store(linear_ref.at[0:1], state_hbm.at[0:1])
    store(state_one, state_hbm.at[1:SPLIT])
    store(gradient_one, gradient_hbm.at[1:SPLIT])
    store(state_two, state_hbm.at[SPLIT:LEV])
    store(gradient_two, gradient_hbm.at[SPLIT:LEV])
    side = side_column(0, HALO, from_west_ref[...], from_east_ref[...])
    f = sweep(extend(adj_ref[...], halo_ref[...], side), c_east_ref[...], c_north_ref[...])
    top_ref[0] = f[:ROWS, :COLS] + inc_ref[...]
    store(top_ref, gradient_hbm.at[0:1])
    for copy in copies:
        copy.wait()


def across(value):
    return lax.ppermute(value, "comp", [(0, 1), (1, 0)])


def along(head, tail, mirror):
    n, m = lax.axis_size("lat"), lax.axis_size("lon")
    return (
        lax.ppermute(tail, "lat", [(i, (i + 1) % n) for i in range(n)]),
        lax.ppermute(head, "lat", [((i + 1) % n, i) for i in range(n)]),
        lax.ppermute(mirror, "lon", [(i, m - 1 - i) for i in range(m)]),
    )


def around(east, west):
    n = lax.axis_size("lon")
    return (
        lax.ppermute(east, "lon", [(i, (i + 1) % n) for i in range(n)]),
        lax.ppermute(west, "lon", [((i + 1) % n, i) for i in range(n)]),
    )


def exchange(slots):
    return lax.all_to_all(slots, "lat", 0, 0, tiled=True)


def local(
    increment, diffusivity, innovation, land_mask, pull_cells, put_cells, pull_weight, pull_count
):
    inc, diff, innov = increment[0], diffusivity[0], innovation[0]
    plane = sds(ROWS, COLS)
    pair = sds(2, ROWS, COLS)
    field = sds(LEV, ROWS, COLS)
    slots = sds(BANDS, 8, 128)
    smem = pl.BlockSpec(memory_space=pltpu.SMEM)
    vmem = pl.BlockSpec(memory_space=pltpu.VMEM)
    params = pltpu.CompilerParams(vmem_limit_bytes=48 << 20)
    barrier = lax.optimization_barrier

    edge = sds(EDGES, 8, COLS)
    cells = jax.ShapeDtypeStruct(slots.shape, I32)
    *edges, mask, other_mask, cells = pl.pallas_call(
        first_pack,
        out_shape=(edge, edge, edge, plane, plane, cells),
        in_specs=[pl.BlockSpec(memory_space=pltpu.HBM)] * 5,
        out_specs=(vmem,) * 6,
        scratch_shapes=[
            pltpu.VMEM((LEV, ROWS, COLS), F32),
            pltpu.VMEM((ROWS, COLS), I32),
            pltpu.VMEM((BANDS, CAP), I32),
            pltpu.SemaphoreType.DMA((8,)),
        ],
        name="first_pack",
        compiler_params=params,
    )(
        *(
            pltpu.with_memory_space_constraint(x, pltpu.HBM)
            for x in (inc, diff, innov, land_mask, pull_cells.reshape(BANDS, CAP))
        )
    )
    pulled = exchange(across(cells))
    packed = sds(32, 256)
    halo, innov_halo, east, west = call(
        first_columns, (sds(FIELDS, 16, COLS), sds(LEV, 8, COLS), packed, packed), "first_columns"
    )(inc, diff, innov, mask, *along(*edges))

    put, weight, east, west = barrier(
        (put_cells.reshape(BANDS, CAP), pull_weight.reshape(BANDS, CAP), east, west)
    )
    received = across(
        pl.pallas_call(
            receive_kernel,
            out_shape=sds(2, BANDS, 8, 128),
            in_specs=[smem, vmem, vmem],
            out_specs=vmem,
            name="receive",
            compiler_params=params,
        )(pull_count.reshape(1, BANDS), put, weight)
    )
    from_west, from_east = around(east, west)
    wide = sds(XR, XC)
    state, surface, c_east, c_north = call(
        first_surface, (pair, plane, wide, wide), "first_surface"
    )(inc, diff, innov, mask, halo, from_west, from_east)
    hbm = pl.BlockSpec(memory_space=pltpu.HBM)
    groups = [pltpu.VMEM((BANDS, 8, 128), F32), pltpu.SemaphoreType.DMA((BANDS // GROUP,))]
    sent = pl.pallas_call(
        gather_kernel,
        out_shape=slots,
        in_specs=[vmem] * 2,
        out_specs=hbm,
        scratch_shapes=groups,
        name="gather_slots",
        compiler_params=params,
    )(pulled, surface)

    sent, halo, state = barrier((sent, halo, state))
    values = exchange(sent)
    state = across(state)
    halo8, west8, east8 = halo, from_west, from_east

    def levels(low, high, name):
        some = sds(high - low, ROWS, COLS)
        wide8 = pltpu.VMEM((32, XC), F32)
        return call(rest_levels(low, high), (some, some), name, [wide8, wide8], nbytes=12000000)

    rest_one = levels(1, SPLIT, "rest_one")(
        inc, diff, innov, mask, halo8, innov_halo, west8, east8
    )

    values, *rest_one = barrier((values, *rest_one))
    acc = pltpu.VMEM((128, 128), F32)
    linear, outgoing = pl.pallas_call(
        couple_kernel,
        out_shape=(pair, slots),
        in_specs=[vmem] * 4,
        out_specs=(vmem, hbm),
        scratch_shapes=[acc, pltpu.VMEM((ROWS, COLS), F32), *groups],
        name="couple",
        compiler_params=params,
    )(values, received, other_mask, state)

    outgoing, linear, halo8 = barrier((outgoing, linear, halo8))
    back = exchange(outgoing)
    linear = across(linear)
    rest_two = levels(SPLIT, LEV, "rest_two")(
        inc, diff, innov, mask, halo8, innov_halo, west8, east8
    )

    back, *rest_two = barrier((back, *rest_two))
    returned = call(collect_kernel, plane, "collect", [acc])(back, pulled)
    edge = sds(1, 8, COLS)
    adj, *edges = call(second_pack, (plane, edge, edge, edge), "second_pack")(
        linear, mask, returned
    )
    packed = sds(XR, 128)
    south, north, fold = along(*edges)
    halo, east, west = call(second_columns, (sds(8, COLS), packed, packed), "second_columns")(
        adj, fold, south, north
    )
    from_west, from_east = around(east, west)
    state, gradient = pl.pallas_call(
        second_surface,
        out_shape=(field, field),
        in_specs=[vmem] * 12,
        out_specs=(hbm, hbm),
        scratch_shapes=[pltpu.VMEM((1, ROWS, COLS), F32), pltpu.SemaphoreType.DMA((6,))],
        name="second_surface",
        compiler_params=params,
    )(
        adj, halo, from_west, from_east, c_east, c_north, inc[0], linear, *rest_one, *rest_two
    )
    return (state[None], gradient[None])


def solution(mesh):
    placed = (
        P("comp", None, "lat", "lon"),
        P("comp", None, "lat", "lon"),
        P("comp", None, "lat", "lon"),
        P("lat", "lon"),
        P("comp", "lat", "lon", None, None),
        P("comp", "lat", "lon", None, None),
        P("comp", "lat", "lon", None, None),
        P("comp", "lat", "lon", None),
    )
    return jax.shard_map(
        local,
        mesh=mesh,
        in_specs=placed,
        out_specs=(P("comp", None, "lat", "lon"), P("comp", None, "lat", "lon")),
        check_vma=False,
    )
```
